32 devices in a mesh: ctx: 16 (over z, y, core), head: 2 (over x).
Axes of the slice: x: 2, y: 2, z: 4, core: 2. Of those that a mesh axis runs over, the one named last changes fastest.
Arguments:
- loader_query_rows: bfloat16 [6144, 8192], P(('ctx', 'head')), may hold values from -6 to 6
- loader_key_rows: bfloat16 [6144, 1024], P(('ctx', 'head')), may hold values from -6 to 6
- loader_value_rows: bfloat16 [6144, 1024], P(('ctx', 'head')), may hold values from -6 to 6
- output_gradient_rows: bfloat16 [6144, 8192], P(('ctx', 'head')), may hold values from -6 to 6
- doc_blocks: int32 [2, 3], replicated, may hold values from 1 to 16, as said below
- block_perm: int32 [48], replicated, may hold values from 0 to 47, as said below
Outputs:
- attn_out: bfloat16 [6144, 8192], P('ctx', 'head')
- grad_query: bfloat16 [6144, 8192], P('ctx', 'head')
- key_gradient: bfloat16 [6144, 1024], P('ctx', 'head')
- value_gradient: bfloat16 [6144, 1024], P('ctx', 'head')
The draws below stay inside these ranges and needn't reach their ends.
Inputs may be any that keep to these rules, and one draw needn't show every extreme that they name: doc_blocks[g] lists in order the lengths, in blocks, of the documents that fill row blocks g * 24 to (g + 1) * 24 - 1 of the packed row; each row sums to 24 and holds one length equal to 16. block_perm is a permutation that maps the blocks of each aligned span of 24 blocks onto the same span.
All inputs are finite; a program needn't handle non-finite values.
Results may differ from the reference program's by a relative error of at most 0.012.
The reference program's roundings to bfloat16 on the way count: a program that leaves them out, or rounds other values in their place, can miss the bound.
Values may be sent and summed in bfloat16 or wider, within the bound.
A program may use at most 192 MiB of HBM per device.

```python
import jax
import jax.numpy as jnp
from jax import lax

QUERY_HEADS = 64
KEY_VALUE_HEADS = 8
HEAD_SIZE = 128
MASK_BLOCK_SIZE = 128
GROUP_DEV = 8
DOCS_G = 3
PACKED_LENGTH = 6144
ROW_BLOCK_COUNT = 48
GROUP_BLOCKS = 24
MOST = 16
NGROUP = 2


def doc_layout(key):
    base_key = jax.random.fold_in(key, 7001)
    others = DOCS_G - 1
    extra_blocks = GROUP_BLOCKS - MOST - others
    lanes = jnp.arange(others, dtype=jnp.int32)

    def spread_one(step_index, counts):
        step_key = jax.random.fold_in(base_key, step_index)
        rank_scores = jax.random.randint(step_key, (NGROUP, others), 0, 1024) * others + lanes[None, :]
        rank_scores = jnp.where(counts >= MOST, -1, rank_scores)
        chosen = jnp.argmax(rank_scores, axis=1)
        return counts + (lanes[None, :] == chosen[:, None]).astype(jnp.int32)
    counts = lax.fori_loop(0, extra_blocks, spread_one, jnp.ones((NGROUP, others), jnp.int32))
    lengths_all = jnp.concatenate([counts, jnp.full((NGROUP, 1), MOST, jnp.int32)], axis=1)
    order_key = jax.random.fold_in(base_key, 99991)
    shuffle = jax.random.randint(order_key, (NGROUP, DOCS_G), 0, 4096) * DOCS_G + jnp.arange(DOCS_G, dtype=jnp.int32)[None, :]
    rank_order = jnp.argsort(shuffle, axis=1)
    return jnp.take_along_axis(lengths_all, rank_order, axis=1).astype(jnp.int32)


def draw_doc_blocks(key, part):
    return doc_layout(key)


def draw_block_perm(key, part):
    lengths = doc_layout(key)
    doc_ends = jnp.cumsum(lengths, axis=1).astype(jnp.int32)
    firsts = doc_ends - lengths
    local_blocks = jnp.arange(GROUP_BLOCKS, dtype=jnp.int32)
    first_of = jnp.max(jnp.where(firsts[:, None, :] <= local_blocks[None, :, None], firsts[:, None, :], 0), axis=2)
    block_work = local_blocks[None, :] - first_of + 1
    tie_key = jax.random.fold_in(key, 7002)
    block_score = block_work * (GROUP_BLOCKS * 1024) + jax.random.randint(tie_key, (NGROUP, GROUP_BLOCKS), 0, 1024) * GROUP_BLOCKS + local_blocks[None, :]
    rank_order = jnp.argsort(-block_score, axis=1)
    lane_index = local_blocks % GROUP_DEV
    sweep_index = local_blocks // GROUP_DEV
    device = jnp.where(sweep_index % 2 == 0, lane_index, GROUP_DEV - 1 - lane_index)
    place_local = device * (GROUP_BLOCKS // GROUP_DEV) + sweep_index
    span_base = jnp.arange(NGROUP, dtype=jnp.int32)[:, None] * GROUP_BLOCKS
    span_rows = jnp.arange(NGROUP, dtype=jnp.int32)[:, None]
    perm_rows = jnp.zeros((NGROUP, GROUP_BLOCKS), jnp.int32).at[span_rows, rank_order].set(span_base + place_local[None, :])
    return jnp.roll(perm_rows, -(GROUP_BLOCKS // 2), axis=1).reshape(-1)


def draw_loader_query_rows(key, part):
    simple_rows = jax.random.normal(jax.random.fold_in(key, 11), (PACKED_LENGTH, QUERY_HEADS * HEAD_SIZE), jnp.float32)
    return jnp.clip(simple_rows, -6.0, 6.0).astype(jnp.bfloat16)


def draw_loader_key_rows(key, part):
    simple_rows = jax.random.normal(jax.random.fold_in(key, 21), (PACKED_LENGTH, KEY_VALUE_HEADS * HEAD_SIZE), jnp.float32)
    return jnp.clip(simple_rows, -6.0, 6.0).astype(jnp.bfloat16)


def levels(rng, shape, shards, least, high):
    def one(axis_at, shards_of):
        heights = jax.random.uniform(jax.random.fold_in(jax.random.fold_in(rng, 6), axis_at), (shards_of,), jnp.float32, least / len(shards), high / len(shards))
        return jnp.repeat(jnp.exp(heights), shape[axis_at] // shards_of).reshape((-1,) + (1,) * (len(shape) - axis_at - 1))

    level = one(*shards[0])
    for cut in shards[1:]:
        level = level * one(*cut)
    return level


def centred(stream_key, dims, deviation, limit, shards=(), kind=jnp.bfloat16):
    values = jax.random.normal(stream_key, dims, jnp.float32) * deviation
    if len(shards) > 0:
        values = levels(stream_key, dims, shards, -0.22, 0.18) * values
    return jnp.clip(values, min=-limit, max=limit).astype(kind)


def setup_inputs(seed: int = 0) -> dict:
    splits = jax.random.split(jax.random.key(seed), 7)
    loader_query_rows = draw_loader_query_rows(jax.random.fold_in(splits[6], 71), 0)
    loader_key_rows = draw_loader_key_rows(jax.random.fold_in(splits[6], 71), 0)
    loader_value_rows = centred(splits[2], (PACKED_LENGTH, KEY_VALUE_HEADS * HEAD_SIZE), 1.0, 6.0, ((0, 32),))
    output_gradient_rows = centred(splits[3], (PACKED_LENGTH, QUERY_HEADS * HEAD_SIZE), 1.0, 6.0, ((0, 32),))
    doc_blocks = draw_doc_blocks(jax.random.fold_in(splits[6], 71), 0)
    block_perm = draw_block_perm(jax.random.fold_in(splits[6], 71), 0)
    return dict(loader_query_rows=loader_query_rows, loader_key_rows=loader_key_rows, loader_value_rows=loader_value_rows, output_gradient_rows=output_gradient_rows, doc_blocks=doc_blocks, block_perm=block_perm)


MASKED_LOGIT = -1e30


def doc_first(doc_blocks, total_blocks):
    doc_ends = jnp.cumsum(doc_blocks, axis=1).astype(jnp.int32)
    span_base = jnp.arange(doc_blocks.shape[0], dtype=jnp.int32)[:, None] * GROUP_BLOCKS
    firsts = (span_base + doc_ends - doc_blocks).reshape(-1).astype(jnp.int32)
    blocks = jnp.arange(total_blocks, dtype=jnp.int32)
    return jnp.max(jnp.where(firsts[None, :] <= blocks[:, None], firsts[None, :], 0), axis=1).astype(jnp.int32)


def round_low(values):
    return lax.optimization_barrier(values.astype(jnp.bfloat16)).astype(jnp.float32)


def rotate_rows(array, shift):
    blocked = array.reshape(NGROUP, GROUP_BLOCKS, MASK_BLOCK_SIZE, array.shape[1])
    return jnp.roll(blocked, shift, axis=1).reshape(array.shape)


def reference(loader_query_rows, loader_key_rows, loader_value_rows, output_gradient_rows, doc_blocks, block_perm):
    query_group_ratio = QUERY_HEADS // KEY_VALUE_HEADS
    logit_scale = HEAD_SIZE ** -0.5
    half_span = GROUP_BLOCKS // 2
    firsts = doc_first(doc_blocks, ROW_BLOCK_COUNT)
    query_matrix = rotate_rows(loader_query_rows, half_span).reshape(ROW_BLOCK_COUNT, MASK_BLOCK_SIZE, KEY_VALUE_HEADS, query_group_ratio, HEAD_SIZE)
    output_cotangents = rotate_rows(output_gradient_rows, half_span).reshape(ROW_BLOCK_COUNT, MASK_BLOCK_SIZE, KEY_VALUE_HEADS, query_group_ratio, HEAD_SIZE)
    every_key = rotate_rows(loader_key_rows, half_span).reshape(PACKED_LENGTH, KEY_VALUE_HEADS, HEAD_SIZE)
    every_value = rotate_rows(loader_value_rows, half_span).reshape(PACKED_LENGTH, KEY_VALUE_HEADS, HEAD_SIZE)
    window = MOST * MASK_BLOCK_SIZE
    token_query = lax.broadcasted_iota(jnp.int32, (MASK_BLOCK_SIZE, 1, 1, window), 0)
    token_key = lax.broadcasted_iota(jnp.int32, (MASK_BLOCK_SIZE, 1, 1, window), 3)

    def step_number(running_totals, block_index):
        doc_start = firsts[block_index]
        window_start = jnp.maximum(block_index - MOST + 1, 0).astype(jnp.int32)
        key_window = lax.dynamic_slice_in_dim(every_key, window_start * MASK_BLOCK_SIZE, window, 0).astype(jnp.float32)
        value_window = lax.dynamic_slice_in_dim(every_value, window_start * MASK_BLOCK_SIZE, window, 0).astype(jnp.float32)
        query_block = query_matrix[block_index].astype(jnp.float32)
        grad_block = output_cotangents[block_index].astype(jnp.float32)
        key_pos = window_start * MASK_BLOCK_SIZE + token_key
        query_pos = block_index * MASK_BLOCK_SIZE + token_query
        allowed = (key_pos <= query_pos) & (key_pos >= doc_start * MASK_BLOCK_SIZE)
        logits = jnp.einsum("tgrd,kgd->tgrk", query_block, key_window) * logit_scale
        logits = jnp.where(allowed, logits, MASKED_LOGIT)
        row_max = jnp.max(logits, axis=3)
        log_total = row_max + jnp.log(jnp.sum(jnp.exp(logits - row_max[..., None]), axis=3))
        weights = jnp.exp(logits - log_total[..., None])
        weights_low = round_low(weights)
        output_rows = jnp.einsum("tgrk,kgd->tgrd", weights_low, value_window).astype(jnp.bfloat16)
        outputs_wide = lax.optimization_barrier(output_rows).astype(jnp.float32)
        delta_rows = jnp.sum(grad_block * outputs_wide, axis=3)
        value_part = jnp.einsum("tgrk,tgrd->kgd", weights_low, grad_block)
        grad_weights = jnp.einsum("tgrd,kgd->tgrk", grad_block, value_window)
        dlogits = round_low(weights * (grad_weights - delta_rows[..., None]))
        query_gradient = (jnp.einsum("tgrk,kgd->tgrd", dlogits, key_window) * logit_scale).astype(jnp.bfloat16)
        key_part = jnp.einsum("tgrk,tgrd->kgd", dlogits, query_block) * logit_scale
        previous = lax.dynamic_slice_in_dim(running_totals, window_start * MASK_BLOCK_SIZE, window, 1)
        running_totals = lax.dynamic_update_slice_in_dim(running_totals, previous + jnp.stack([key_part, value_part]), window_start * MASK_BLOCK_SIZE, 1)
        return running_totals, (output_rows, query_gradient)

    running_totals, (output_rows, query_gradient) = lax.scan(step_number, jnp.zeros((2, PACKED_LENGTH, KEY_VALUE_HEADS, HEAD_SIZE), jnp.float32), jnp.arange(ROW_BLOCK_COUNT, dtype=jnp.int32))

    def balanced_mapping(array):
        loader_rows = rotate_rows(array, -half_span)
        blocked = loader_rows.reshape(ROW_BLOCK_COUNT, MASK_BLOCK_SIZE, array.shape[1])
        return jnp.zeros_like(blocked).at[block_perm].set(blocked).reshape(PACKED_LENGTH, array.shape[1])

    attn_out = balanced_mapping(output_rows.reshape(PACKED_LENGTH, QUERY_HEADS * HEAD_SIZE))
    grad_query = balanced_mapping(query_gradient.reshape(PACKED_LENGTH, QUERY_HEADS * HEAD_SIZE))
    key_gradient = balanced_mapping(running_totals[0].reshape(PACKED_LENGTH, KEY_VALUE_HEADS * HEAD_SIZE).astype(jnp.bfloat16))
    value_gradient = balanced_mapping(running_totals[1].reshape(PACKED_LENGTH, KEY_VALUE_HEADS * HEAD_SIZE).astype(jnp.bfloat16))
    return (attn_out, grad_query, key_gradient, value_gradient)
```

```python
from functools import partial
import math

import jax
import jax.numpy as jnp
from jax import lax
from jax.experimental import pallas as pl
from jax.experimental.pallas import tpu as pltpu
from jax.sharding import PartitionSpec as P

QUERY_HEADS = 64
KEY_VALUE_HEADS = 8
HEAD_SIZE = 128
MASK_BLOCK_SIZE = 128
GROUP_DEV = 8
GROUP_BLOCKS = 24
MOST = 16

RATIO = QUERY_HEADS // KEY_VALUE_HEADS
MASKED_LOGIT = -1e30
CHUNK = 512
SPAN_TOKENS = GROUP_BLOCKS * MASK_BLOCK_SIZE
LONG_TOKENS = MOST * MASK_BLOCK_SIZE
MESH = pl.DeviceIdType.MESH

SPREAD_ORDER = [13, 5, 9, 15, 7, 11, 12, 4, 8, 14, 6, 10, 1, 3, 2]
GATHER_ORDER = [6, 2, 4, 7, 3, 5, 1]


def enter(peers):
    barrier = pltpu.get_barrier_semaphore()
    for peer in peers:
        pl.semaphore_signal(barrier, inc=1, device_id=peer, device_id_type=MESH)
    pl.semaphore_wait(barrier, len(peers))


def flipped(index, mask, count):
    result, bit = index, 1
    while bit < count:
        if mask & bit:
            result = result + bit - index // bit % 2 * (2 * bit)
        bit *= 2
    return result


def visiting_order(members):
    return SPREAD_ORDER if len(SPREAD_ORDER) == members - 1 else list(range(members - 1, 0, -1))


def dot(left, right):
    return jnp.dot(left, right, preferred_element_type=jnp.float32)


def copy_to(source, target, send_sem, recv_sem, device):
    return pltpu.make_async_remote_copy(
        src_ref=source,
        dst_ref=target,
        send_sem=send_sem,
        recv_sem=recv_sem,
        device_id=device,
        device_id_type=MESH,
    )


def fused_kernel(head_dim, heads, *refs):
    refs = list(refs)

    def take(count):
        taken, refs[:] = refs[:count], refs[count:]
        return taken

    docs_ref, perm_ref, query_ref, grad_ref, key_ref, value_ref = take(6)
    attn_out, query_grad_out, pair_out = take(3)
    query_land, grad_land = take(heads), take(heads)
    (pair_land,) = take(1)
    query_s, grad_s, query_t, grad_t, keys, values, keys_t, values_t = take(8)
    store, out_t, query_grad_t, key_total, value_total, out_s, query_grad_s = take(7)
    attn_place, query_grad_place, pair_place, other, mine = take(5)
    slot_at, source_at, place_at = take(3)
    in_send, in_recv, pair_send, pair_recv, pass_send, pass_recv = take(6)
    out_send, out_recv, part_send, part_recv, swap_sems, local_sems, out_local = take(7)

    members = GROUP_DEV * head_dim
    units, unit, _ = query_ref.shape
    wide = heads * HEAD_SIZE
    block = MASK_BLOCK_SIZE
    per_block = block // unit
    per_chunk = CHUNK // block
    out_rows = SPAN_TOKENS // GROUP_DEV
    sharers = RATIO // heads
    scale = HEAD_SIZE ** (-0.5)
    scale_log2 = scale * math.log2(math.e)

    ctx = lax.axis_index("ctx")
    head = lax.axis_index("head")
    group = ctx // GROUP_DEV
    base = group * GROUP_DEV
    lane = ctx - base
    kind = lane % 2
    own = lane * head_dim + head
    order = visiting_order(members)

    def rows_of(member):
        return pl.ds(member * units, units)

    def head_columns(peer_lane, peer_head, h):
        worker = peer_head * GROUP_DEV + peer_lane
        return pl.ds(pl.multiple_of(worker * wide + h * HEAD_SIZE, HEAD_SIZE), HEAD_SIZE)

    def key_columns(peer_lane, peer_head):
        worker = peer_head * GROUP_DEV + peer_lane
        return pl.ds(
            pl.multiple_of(worker * heads // RATIO * HEAD_SIZE, HEAD_SIZE), HEAD_SIZE
        )

    landing = rows_of(own)
    masks = [(mask, flipped(own, mask, members)) for mask in order]
    peers = [(mask, member, member // head_dim, member % head_dim) for mask, member in masks]
    device = [{"ctx": base + peer_lane, "head": peer_head} for _, _, peer_lane, peer_head in peers]
    sibling = {"ctx": base + flipped(lane, 1, GROUP_DEV), "head": head}

    def own_pair(own_kind):
        return pltpu.make_async_copy(
            (key_ref, value_ref)[own_kind].at[:, :, key_columns(lane, head)],
            pair_land.at[own_kind, landing],
            local_sems.at[2 * heads],
        )

    def pair_copy(step, peer_kind):
        _, _, peer_lane, peer_head = peers[step]
        return copy_to(
            (key_ref, value_ref)[peer_kind].at[:, :, key_columns(peer_lane, peer_head)],
            pair_land.at[peer_kind, landing],
            pair_send.at[step],
            pair_recv.at[step],
            device[step],
        )

    loads = []
    for h in range(heads):
        at = head_columns(lane, head, h)
        for index, (source, target) in enumerate(
            ((query_ref, query_land[h]), (grad_ref, grad_land[h]))
        ):
            load = pltpu.make_async_copy(
                source.at[:, :, at], target.at[landing], local_sems.at[2 * h + index]
            )
            load.start()
            loads.append(load)
    for own_kind in range(2):

        @pl.when(kind == own_kind)
        def _(own_kind=own_kind):
            own_pair(own_kind).start()

    enter(device)
    for own_kind in range(2):

        @pl.when(kind == own_kind)
        def _(own_kind=own_kind):
            for step, (mask, _, _, _) in enumerate(peers):
                pair_copy(step, (own_kind + mask // head_dim) % 2).start()

    head_copies = []
    for h in range(heads):
        copies = []
        for step, (_, _, peer_lane, peer_head) in enumerate(peers):
            at = head_columns(peer_lane, peer_head, h)
            for index, (source, target) in enumerate(
                ((query_ref, query_land[h]), (grad_ref, grad_land[h]))
            ):
                copy = copy_to(
                    source.at[:, :, at],
                    target.at[landing],
                    in_send.at[h, index, step],
                    in_recv.at[h, index, step],
                    device[step],
                )
                copy.start()
                copies.append(copy)
        head_copies.append(copies)

    lengths = [docs_ref[group, i] for i in range(docs_ref.shape[1])]
    starts, start = [], jnp.int32(0)
    for length in lengths:
        starts.append(start)
        start = start + length
    big = jnp.int32(0)
    for length, start in zip(lengths, starts):
        big = big + jnp.where(length == MOST, start, 0)
    other_starts = [
        jnp.where(length == MOST, 0, start - jnp.where(start > big, MOST, 0)) * block
        for length, start in zip(lengths, starts)
    ]

    def loader_of(row_block):
        moved = row_block + GROUP_BLOCKS // 2
        return jnp.where(moved >= GROUP_BLOCKS, moved - GROUP_BLOCKS, moved)

    for slot in range(GROUP_BLOCKS):
        if slot < MOST:
            row_block = big + slot
        else:
            other_block = slot - MOST
            row_block = jnp.where(big <= other_block, slot, other_block)
        source_at[slot] = loader_of(row_block)
    for loader in range(GROUP_BLOCKS):
        row_block = (loader + GROUP_BLOCKS // 2) % GROUP_BLOCKS
        slot = row_block - big
        slot = jnp.where(slot >= MOST, row_block, slot)
        slot_at[loader] = jnp.where(slot < 0, row_block + MOST, slot)

    def find(place, _):
        found = jnp.int32(0)
        for loader in range(GROUP_BLOCKS):
            hit = perm_ref[group * GROUP_BLOCKS + loader] == group * GROUP_BLOCKS + place
            found = jnp.where(hit, slot_at[loader], found)
        place_at[place] = found
        return 0

    lax.fori_loop(0, GROUP_BLOCKS, find, 0)

    key_total[...] = jnp.zeros_like(key_total)
    value_total[...] = jnp.zeros_like(value_total)

    def passing(slot, spot):
        copy = copy_to(
            pair_land.at[kind, spot],
            pair_land.at[kind, spot],
            pass_send.at[slot],
            pass_recv.at[slot],
            sibling,
        )
        copy.start()
        return copy

    pltpu.make_async_copy(
        key_ref.at[:, :, key_columns(lane, head)],
        pair_land.at[kind, landing],
        local_sems.at[2 * heads],
    ).wait()
    passes = [passing(members - 1, landing)]
    pairs = []
    for step, (_, member, _, _) in enumerate(peers):
        pair = copy_to(
            key_ref.at[:, :, key_columns(lane, head)],
            pair_land.at[kind, rows_of(member)],
            pair_send.at[step],
            pair_recv.at[step],
            device[step],
        )
        pair.wait_recv()
        pairs.append(pair)
        passes.append(passing(step, rows_of(member)))
    for copy in passes:
        copy.wait()

    def to_slot(slot):
        return pl.ds(pl.multiple_of(slot * block, block), block)

    def take_pair(slot, _):
        source, target = source_at[slot] * per_block, to_slot(slot)
        for which, flat, turned in ((0, keys, keys_t), (1, values, values_t)):
            rows_in = [pair_land[which, source + part] for part in range(per_block)]
            rows_in = jnp.concatenate(rows_in, axis=0)
            flat[target, :] = rows_in
            turned[:, target] = rows_in.T
        return 0

    lax.fori_loop(0, GROUP_BLOCKS, take_pair, 0)

    token = lax.broadcasted_iota(jnp.int32, (CHUNK, CHUNK), 1)
    key_at = lax.broadcasted_iota(jnp.int32, (CHUNK, CHUNK), 0)

    def tile(first, index, short):
        at = pl.ds(pl.multiple_of(first + index * CHUNK, CHUNK), CHUNK)
        steps = index + 1

        def spot(step):
            return pl.ds(pl.multiple_of(first + step * CHUNK, CHUNK), CHUNK)

        def slot(step):
            return pl.ds(pl.multiple_of(step * CHUNK, CHUNK), CHUNK)

        def blocks(step):
            return pl.ds(first // block + step * per_chunk, per_chunk)

        def blocked(array):
            return array.reshape(per_chunk, block, HEAD_SIZE)

        queries_t = query_t[:, at]
        grads_t = grad_t[:, at]
        column = index * CHUNK + lax.broadcasted_iota(jnp.int32, (1, CHUNK), 1)
        opened = jnp.zeros((1, CHUNK), jnp.int32)
        if short:
            for start in other_starts:
                opened = jnp.maximum(opened, jnp.where(column >= start, start, 0))

        def logits(step, peak, diagonal):
            raw = dot(keys[spot(step), :], queries_t)
            if diagonal:
                allowed = key_at <= token
                if short:
                    allowed = allowed & (key_at >= opened - step * CHUNK)
                raw = jnp.where(allowed, raw, MASKED_LOGIT)
            elif short:
                raw = jnp.where(key_at >= opened - step * CHUNK, raw, MASKED_LOGIT)
            store[slot(step), :] = raw
            return jnp.maximum(peak, jnp.max(raw, axis=0, keepdims=True))

        peak = lax.fori_loop(
            0,
            index,
            lambda step, peak: logits(step, peak, False),
            jnp.full((1, CHUNK), MASKED_LOGIT, jnp.float32),
        )
        peak = logits(index, peak, True) * scale_log2
        out_t[...] = jnp.zeros_like(out_t)

        def mix(step, total):
            mass = jnp.exp2(store[slot(step), :] * scale_log2 - peak)
            store[slot(step), :] = mass
            out_t[...] += dot(values_t[:, spot(step)], mass.astype(jnp.bfloat16))
            return total + jnp.sum(mass, axis=0, keepdims=True)

        total = lax.fori_loop(0, steps, mix, jnp.zeros((1, CHUNK), jnp.float32))
        share = 1.0 / total
        out = (out_t[...] * share).astype(jnp.bfloat16)
        delta = jnp.sum(
            out.astype(jnp.float32) * grads_t.astype(jnp.float32), axis=0, keepdims=True
        )
        out_s[blocks(index)] = blocked(out.T)
        query_grad_t[...] = jnp.zeros_like(query_grad_t)

        def back(step, carry):
            weights = store[slot(step), :] * share
            value_total[blocks(step)] += blocked(dot(weights.astype(jnp.bfloat16), grad_s[at, :]))
            grad_weights = dot(values[spot(step), :], grads_t)
            dlogits = (weights * (grad_weights - delta)).astype(jnp.bfloat16)
            key_total[blocks(step)] += blocked(dot(dlogits, query_s[at, :]))
            query_grad_t[...] += dot(keys_t[:, spot(step)], dlogits)
            return carry

        lax.fori_loop(0, steps, back, 0)
        query_grad_s[blocks(index)] = blocked((query_grad_t[...] * scale).astype(jnp.bfloat16).T)

    own_columns = lane * wide
    out_peers = [flipped(lane, mask, GROUP_DEV) for mask in GATHER_ORDER]
    out_device = [{"ctx": base + peer, "head": head} for peer in out_peers]

    def taken(peer):
        return pl.ds(pl.multiple_of(peer * out_rows, 16), out_rows)

    sent, stores = [], []
    for h in range(heads):
        for load in loads[2 * h : 2 * h + 2]:
            load.wait()
        for copy in head_copies[h]:
            copy.wait_recv()

        def take_head(slot, _, h=h):
            source, target = source_at[slot] * per_block, to_slot(slot)
            for land, flat, turned in (
                (query_land[h], query_s, query_t),
                (grad_land[h], grad_s, grad_t),
            ):
                rows_in = [land[source + part] for part in range(per_block)]
                rows_in = jnp.concatenate(rows_in, axis=0)
                flat[target, :] = rows_in
                turned[:, target] = rows_in.T
            return 0

        lax.fori_loop(0, GROUP_BLOCKS, take_head, 0)

        def long_tile(index, _):
            tile(0, index, False)
            return 0

        def short_tile(index, _):
            tile(LONG_TOKENS, index, True)
            return 0

        lax.fori_loop(0, (SPAN_TOKENS - LONG_TOKENS) // CHUNK, short_tile, 0)
        lax.fori_loop(0, LONG_TOKENS // CHUNK, long_tile, 0)

        def put_head(place, _, h=h):
            source, target = place_at[place], to_slot(place)
            attn_place[h, target, :] = out_s[source]
            query_grad_place[h, target, :] = query_grad_s[source]
            return 0

        lax.fori_loop(0, GROUP_BLOCKS, put_head, 0)

        out_at = pl.ds(pl.multiple_of(own_columns + h * HEAD_SIZE, HEAD_SIZE), HEAD_SIZE)
        for index, (source, target) in enumerate(
            ((attn_place, attn_out), (query_grad_place, query_grad_out))
        ):
            for step, peer in enumerate(out_peers):
                copy = copy_to(
                    source.at[h, taken(peer), :],
                    target.at[:, out_at],
                    out_send.at[h, index, step],
                    out_recv.at[h, index, step],
                    out_device[step],
                )
                copy.start()
                sent.append(copy)
            keep = pltpu.make_async_copy(
                source.at[h, taken(lane), :], target.at[:, out_at], out_local.at[2 * h + index]
            )
            keep.start()
            stores.append(keep)

    def put_pair(place, _):
        source, target = place_at[place], to_slot(place)
        pair_place[0, target, :] = (key_total[source] * scale).astype(jnp.bfloat16)
        pair_place[1, target, :] = value_total[source].astype(jnp.bfloat16)
        return 0

    lax.fori_loop(0, GROUP_BLOCKS, put_pair, 0)
    swap = copy_to(pair_place.at[1 - kind], other, swap_sems.at[0], swap_sems.at[1], sibling)
    swap.start()
    swap.wait()

    def add_pair(place, _):
        at = to_slot(place)
        total = pair_place[kind, at, :].astype(jnp.float32) + other[at, :].astype(jnp.float32)
        mine[at, :] = total.astype(jnp.bfloat16)
        return 0

    lax.fori_loop(0, GROUP_BLOCKS, add_pair, 0)
    pair_at = pl.ds(pl.multiple_of(lane // sharers * HEAD_SIZE, HEAD_SIZE), HEAD_SIZE)
    pair_landing = pair_out.at[kind, lane % sharers // 2, :, pair_at]
    keep = pltpu.make_async_copy(mine.at[taken(lane), :], pair_landing, out_local.at[2 * heads])
    keep.start()
    stores.append(keep)
    for step, peer in enumerate(out_peers):
        copy = copy_to(
            mine.at[taken(peer), :],
            pair_landing,
            part_send.at[step],
            part_recv.at[step],
            out_device[step],
        )
        copy.start()
        sent.append(copy)
    for keep in stores:
        keep.wait()
    for pair in pairs:
        pair.wait_send()
    for copies in head_copies:
        for copy in copies:
            copy.wait_send()
    for copy in sent:
        copy.wait()


def fused(head_dim, query, grad, key, value, doc_blocks, block_perm):
    rows, width = query.shape
    unit = math.gcd(rows, MASK_BLOCK_SIZE)
    members = GROUP_DEV * head_dim
    wide = width // members
    heads = wide // HEAD_SIZE
    sharers = RATIO // heads
    tokens = rows * members
    out_rows = tokens // GROUP_DEV
    any_spec = pl.BlockSpec(memory_space=pl.ANY)
    smem = pl.BlockSpec(memory_space=pltpu.SMEM)

    def low(*shape):
        return pltpu.VMEM(shape, jnp.bfloat16)

    def full(*shape):
        return pltpu.VMEM(shape, jnp.float32)

    dma = pltpu.SemaphoreType.DMA
    flat, turned = (tokens, HEAD_SIZE), (HEAD_SIZE, tokens)
    landed = (tokens // unit, unit, HEAD_SIZE)
    blocked = (tokens // MASK_BLOCK_SIZE, MASK_BLOCK_SIZE, HEAD_SIZE)
    query, grad, key, value = (
        array.reshape(rows // unit, unit, -1) for array in (query, grad, key, value)
    )
    return pl.pallas_call(
        partial(fused_kernel, head_dim, heads),
        out_shape=[
            jax.ShapeDtypeStruct((out_rows, wide * GROUP_DEV), jnp.bfloat16),
            jax.ShapeDtypeStruct((out_rows, wide * GROUP_DEV), jnp.bfloat16),
            jax.ShapeDtypeStruct(
                (2, sharers // 2, out_rows, HEAD_SIZE * GROUP_DEV // sharers), jnp.bfloat16
            ),
        ],
        in_specs=[smem, smem] + [any_spec] * 4,
        out_specs=[any_spec] * 3,
        scratch_shapes=[low(*landed) for _ in range(2 * heads)]
        + [low(2, *landed)]
        + [low(*flat), low(*flat), low(*turned), low(*turned)] * 2
        + [full(LONG_TOKENS, CHUNK), full(HEAD_SIZE, CHUNK), full(HEAD_SIZE, CHUNK)]
        + [full(*blocked), full(*blocked), low(*blocked), low(*blocked)]
        + [low(heads, *flat), low(heads, *flat), low(2, *flat), low(*flat), low(*flat)]
        + [pltpu.SMEM((GROUP_BLOCKS,), jnp.int32)] * 3
        + [dma((heads, 2, members - 1))] * 2
        + [dma((members - 1,))] * 2
        + [dma((members,))] * 2
        + [dma((heads, 2, GROUP_DEV - 1))] * 2
        + [dma((GROUP_DEV - 1,))] * 2
        + [dma((2,)), dma((2 * heads + 1,)), dma((2 * heads + 1,))],
        compiler_params=pltpu.CompilerParams(
            collective_id=0, has_side_effects=True, vmem_limit_bytes=60 * 1024 * 1024
        ),
        name="fused",
    )(doc_blocks, block_perm, query, grad, key, value)


def body(head_dim, query_rows, key_rows, value_rows, grad_rows, doc_blocks, block_perm):
    attn, query_grad, parts = fused(
        head_dim, query_rows, grad_rows, key_rows, value_rows, doc_blocks, block_perm
    )
    if parts.shape[1] > 1:
        parts = jnp.sum(parts.astype(jnp.float32), axis=1).astype(jnp.bfloat16)
    else:
        parts = parts[:, 0]
    return attn, query_grad, parts[0], parts[1]


def solution(mesh):
    split = P(("ctx", "head"), None)
    out_spec = P("ctx", "head")
    return jax.shard_map(
        partial(body, mesh.shape["head"]),
        mesh=mesh,
        in_specs=(split, split, split, split, P(), P()),
        out_specs=(out_spec,) * 4,
        check_vma=False,
    )
```

```python
from functools import partial
import math

import jax
import jax.numpy as jnp
from jax import lax
from jax.experimental import pallas as pl
from jax.experimental.pallas import tpu as pltpu
from jax.sharding import PartitionSpec as P

QUERY_HEADS = 64
KEY_VALUE_HEADS = 8
HEAD_SIZE = 128
MASK_BLOCK_SIZE = 128
GROUP_DEV = 8
GROUP_BLOCKS = 24
MOST = 16

RATIO = QUERY_HEADS // KEY_VALUE_HEADS
MASKED_LOGIT = -1e30
CHUNK = 512
SPAN_TOKENS = GROUP_BLOCKS * MASK_BLOCK_SIZE
LONG_TOKENS = MOST * MASK_BLOCK_SIZE
MESH = pl.DeviceIdType.MESH

SPREAD_ORDER = [13, 4, 8, 15, 6, 10, 5, 12, 9, 7, 14, 11, 1, 3, 2]
GATHER_ORDER = [6, 2, 4, 7, 3, 5, 1]


def enter(peers):
    barrier = pltpu.get_barrier_semaphore()
    for peer in peers:
        pl.semaphore_signal(barrier, inc=1, device_id=peer, device_id_type=MESH)
    pl.semaphore_wait(barrier, len(peers))


def flipped(index, mask, count):
    result, bit = index, 1
    while bit < count:
        if mask & bit:
            result = result + bit - index // bit % 2 * (2 * bit)
        bit *= 2
    return result


def visiting_order(members):
    return SPREAD_ORDER if len(SPREAD_ORDER) == members - 1 else list(range(members - 1, 0, -1))


def dot(left, right):
    return jnp.dot(left, right, preferred_element_type=jnp.float32)


def copy_to(source, target, send_sem, recv_sem, device):
    return pltpu.make_async_remote_copy(
        src_ref=source,
        dst_ref=target,
        send_sem=send_sem,
        recv_sem=recv_sem,
        device_id=device,
        device_id_type=MESH,
    )


def fused_kernel(head_dim, heads, *refs):
    refs = list(refs)

    def take(count):
        taken, refs[:] = refs[:count], refs[count:]
        return taken

    docs_ref, perm_ref, query_ref, grad_ref, key_ref, value_ref = take(6)
    attn_out, query_grad_out, pair_out = take(3)
    query_land, grad_land = take(heads), take(heads)
    (pair_land,) = take(1)
    query_s, grad_s, query_t, grad_t, keys, values, keys_t, values_t = take(8)
    store, out_t, query_grad_t, key_total, value_total, out_s, query_grad_s = take(7)
    attn_place, query_grad_place, pair_place, other, mine = take(5)
    slot_at, source_at, place_at = take(3)
    in_send, in_recv, pair_send, pair_recv, pass_send, pass_recv = take(6)
    out_send, out_recv, part_send, part_recv, swap_sems, local_sems, out_local = take(7)

    members = GROUP_DEV * head_dim
    units, unit, _ = query_ref.shape
    wide = heads * HEAD_SIZE
    block = MASK_BLOCK_SIZE
    per_block = block // unit
    per_chunk = CHUNK // block
    out_rows = SPAN_TOKENS // GROUP_DEV
    sharers = RATIO // heads
    scale = HEAD_SIZE ** (-0.5)
    scale_log2 = scale * math.log2(math.e)

    ctx = lax.axis_index("ctx")
    head = lax.axis_index("head")
    group = ctx // GROUP_DEV
    base = group * GROUP_DEV
    lane = ctx - base
    kind = lane % 2
    own = lane * head_dim + head
    order = visiting_order(members)

    def rows_of(member):
        return pl.ds(member * units, units)

    def head_columns(peer_lane, peer_head, h):
        worker = peer_head * GROUP_DEV + peer_lane
        return pl.ds(pl.multiple_of(worker * wide + h * HEAD_SIZE, HEAD_SIZE), HEAD_SIZE)

    def key_columns(peer_lane, peer_head):
        worker = peer_head * GROUP_DEV + peer_lane
        return pl.ds(
            pl.multiple_of(worker * heads // RATIO * HEAD_SIZE, HEAD_SIZE), HEAD_SIZE
        )

    landing = rows_of(own)
    masks = [(mask, flipped(own, mask, members)) for mask in order]
    peers = [(mask, member, member // head_dim, member % head_dim) for mask, member in masks]
    device = [{"ctx": base + peer_lane, "head": peer_head} for _, _, peer_lane, peer_head in peers]
    sibling = {"ctx": base + flipped(lane, 1, GROUP_DEV), "head": head}

    def own_pair(own_kind):
        return pltpu.make_async_copy(
            (key_ref, value_ref)[own_kind].at[:, :, key_columns(lane, head)],
            pair_land.at[own_kind, landing],
            local_sems.at[2 * heads],
        )

    def pair_copy(step, peer_kind):
        _, _, peer_lane, peer_head = peers[step]
        return copy_to(
            (key_ref, value_ref)[peer_kind].at[:, :, key_columns(peer_lane, peer_head)],
            pair_land.at[peer_kind, landing],
            pair_send.at[step],
            pair_recv.at[step],
            device[step],
        )

    loads = []
    for h in range(heads):
        at = head_columns(lane, head, h)
        for index, (source, target) in enumerate(
            ((query_ref, query_land[h]), (grad_ref, grad_land[h]))
        ):
            load = pltpu.make_async_copy(
                source.at[:, :, at], target.at[landing], local_sems.at[2 * h + index]
            )
            load.start()
            loads.append(load)
    for own_kind in range(2):

        @pl.when(kind == own_kind)
        def _(own_kind=own_kind):
            own_pair(own_kind).start()

    enter(device)
    for own_kind in range(2):

        @pl.when(kind == own_kind)
        def _(own_kind=own_kind):
            for step, (mask, _, _, _) in enumerate(peers):
                pair_copy(step, (own_kind + mask // head_dim) % 2).start()

    head_copies = []
    for h in range(heads):
        copies = []
        for step, (_, _, peer_lane, peer_head) in enumerate(peers):
            at = head_columns(peer_lane, peer_head, h)
            for index, (source, target) in enumerate(
                ((query_ref, query_land[h]), (grad_ref, grad_land[h]))
            ):
                copy = copy_to(
                    source.at[:, :, at],
                    target.at[landing],
                    in_send.at[h, index, step],
                    in_recv.at[h, index, step],
                    device[step],
                )
                copy.start()
                copies.append(copy)
        head_copies.append(copies)

    lengths = [docs_ref[group, i] for i in range(docs_ref.shape[1])]
    starts, start = [], jnp.int32(0)
    for length in lengths:
        starts.append(start)
        start = start + length
    big = jnp.int32(0)
    for length, start in zip(lengths, starts):
        big = big + jnp.where(length == MOST, start, 0)
    other_starts = [
        jnp.where(length == MOST, 0, start - jnp.where(start > big, MOST, 0)) * block
        for length, start in zip(lengths, starts)
    ]

    def loader_of(row_block):
        moved = row_block + GROUP_BLOCKS // 2
        return jnp.where(moved >= GROUP_BLOCKS, moved - GROUP_BLOCKS, moved)

    for slot in range(GROUP_BLOCKS):
        if slot < MOST:
            row_block = big + slot
        else:
            other_block = slot - MOST
            row_block = jnp.where(big <= other_block, slot, other_block)
        source_at[slot] = loader_of(row_block)
    for loader in range(GROUP_BLOCKS):
        row_block = (loader + GROUP_BLOCKS // 2) % GROUP_BLOCKS
        slot = row_block - big
        slot = jnp.where(slot >= MOST, row_block, slot)
        slot_at[loader] = jnp.where(slot < 0, row_block + MOST, slot)

    def find(place, _):
        found = jnp.int32(0)
        for loader in range(GROUP_BLOCKS):
            hit = perm_ref[group * GROUP_BLOCKS + loader] == group * GROUP_BLOCKS + place
            found = jnp.where(hit, slot_at[loader], found)
        place_at[place] = found
        return 0

    lax.fori_loop(0, GROUP_BLOCKS, find, 0)

    key_total[...] = jnp.zeros_like(key_total)
    value_total[...] = jnp.zeros_like(value_total)

    def passing(slot, spot):
        copy = copy_to(
            pair_land.at[kind, spot],
            pair_land.at[kind, spot],
            pass_send.at[slot],
            pass_recv.at[slot],
            sibling,
        )
        copy.start()
        return copy

    pltpu.make_async_copy(
        key_ref.at[:, :, key_columns(lane, head)],
        pair_land.at[kind, landing],
        local_sems.at[2 * heads],
    ).wait()
    passes = [passing(members - 1, landing)]
    pairs = []
    for step, (_, member, _, _) in enumerate(peers):
        pair = copy_to(
            key_ref.at[:, :, key_columns(lane, head)],
            pair_land.at[kind, rows_of(member)],
            pair_send.at[step],
            pair_recv.at[step],
            device[step],
        )
        pair.wait_recv()
        pairs.append(pair)
        passes.append(passing(step, rows_of(member)))
    for copy in passes:
        copy.wait()

    def to_slot(slot):
        return pl.ds(pl.multiple_of(slot * block, block), block)

    def take_pair(slot, _):
        source, target = source_at[slot] * per_block, to_slot(slot)
        for which, flat, turned in ((0, keys, keys_t), (1, values, values_t)):
            rows_in = [pair_land[which, source + part] for part in range(per_block)]
            rows_in = jnp.concatenate(rows_in, axis=0)
            flat[target, :] = rows_in
            turned[:, target] = rows_in.T
        return 0

    lax.fori_loop(0, GROUP_BLOCKS, take_pair, 0)

    token = lax.broadcasted_iota(jnp.int32, (CHUNK, CHUNK), 1)
    key_at = lax.broadcasted_iota(jnp.int32, (CHUNK, CHUNK), 0)

    def tile(first, index, short):
        at = pl.ds(pl.multiple_of(first + index * CHUNK, CHUNK), CHUNK)
        steps = index + 1

        def spot(step):
            return pl.ds(pl.multiple_of(first + step * CHUNK, CHUNK), CHUNK)

        def slot(step):
            return pl.ds(pl.multiple_of(step * CHUNK, CHUNK), CHUNK)

        def blocks(step):
            return pl.ds(first // block + step * per_chunk, per_chunk)

        def blocked(array):
            return array.reshape(per_chunk, block, HEAD_SIZE)

        queries_t = query_t[:, at]
        grads_t = grad_t[:, at]
        column = index * CHUNK + lax.broadcasted_iota(jnp.int32, (1, CHUNK), 1)
        opened = jnp.zeros((1, CHUNK), jnp.int32)
        if short:
            for start in other_starts:
                opened = jnp.maximum(opened, jnp.where(column >= start, start, 0))

        def logits(step, peak, diagonal):
            raw = dot(keys[spot(step), :], queries_t)
            if diagonal:
                allowed = key_at <= token
                if short:
                    allowed = allowed & (key_at >= opened - step * CHUNK)
                raw = jnp.where(allowed, raw, MASKED_LOGIT)
            elif short:
                raw = jnp.where(key_at >= opened - step * CHUNK, raw, MASKED_LOGIT)
            store[slot(step), :] = raw
            return jnp.maximum(peak, jnp.max(raw, axis=0, keepdims=True))

        peak = lax.fori_loop(
            0,
            index,
            lambda step, peak: logits(step, peak, False),
            jnp.full((1, CHUNK), MASKED_LOGIT, jnp.float32),
        )
        peak = logits(index, peak, True) * scale_log2
        out_t[...] = jnp.zeros_like(out_t)

        def mix(step, total):
            mass = jnp.exp2(store[slot(step), :] * scale_log2 - peak)
            store[slot(step), :] = mass
            out_t[...] += dot(values_t[:, spot(step)], mass.astype(jnp.bfloat16))
            return total + jnp.sum(mass, axis=0, keepdims=True)

        total = lax.fori_loop(0, steps, mix, jnp.zeros((1, CHUNK), jnp.float32))
        share = 1.0 / total
        out = (out_t[...] * share).astype(jnp.bfloat16)
        delta = jnp.sum(
            out.astype(jnp.float32) * grads_t.astype(jnp.float32), axis=0, keepdims=True
        )
        out_s[blocks(index)] = blocked(out.T)
        query_grad_t[...] = jnp.zeros_like(query_grad_t)

        def back(step, carry):
            weights = store[slot(step), :] * share
            value_total[blocks(step)] += blocked(dot(weights.astype(jnp.bfloat16), grad_s[at, :]))
            grad_weights = dot(values[spot(step), :], grads_t)
            dlogits = (weights * (grad_weights - delta)).astype(jnp.bfloat16)
            key_total[blocks(step)] += blocked(dot(dlogits, query_s[at, :]))
            query_grad_t[...] += dot(keys_t[:, spot(step)], dlogits)
            return carry

        lax.fori_loop(0, steps, back, 0)
        query_grad_s[blocks(index)] = blocked((query_grad_t[...] * scale).astype(jnp.bfloat16).T)

    own_columns = lane * wide
    out_peers = [flipped(lane, mask, GROUP_DEV) for mask in GATHER_ORDER]
    out_device = [{"ctx": base + peer, "head": head} for peer in out_peers]

    def taken(peer):
        return pl.ds(pl.multiple_of(peer * out_rows, 16), out_rows)

    sent, stores = [], []
    for h in range(heads):
        for load in loads[2 * h : 2 * h + 2]:
            load.wait()
        for copy in head_copies[h]:
            copy.wait_recv()

        def take_head(slot, _, h=h):
            source, target = source_at[slot] * per_block, to_slot(slot)
            for land, flat, turned in (
                (query_land[h], query_s, query_t),
                (grad_land[h], grad_s, grad_t),
            ):
                rows_in = [land[source + part] for part in range(per_block)]
                rows_in = jnp.concatenate(rows_in, axis=0)
                flat[target, :] = rows_in
                turned[:, target] = rows_in.T
            return 0

        lax.fori_loop(0, GROUP_BLOCKS, take_head, 0)

        def long_tile(index, _):
            tile(0, index, False)
            return 0

        def short_tile(index, _):
            tile(LONG_TOKENS, index, True)
            return 0

        lax.fori_loop(0, (SPAN_TOKENS - LONG_TOKENS) // CHUNK, short_tile, 0)
        lax.fori_loop(0, LONG_TOKENS // CHUNK, long_tile, 0)

        def put_head(place, _, h=h):
            source, target = place_at[place], to_slot(place)
            attn_place[h, target, :] = out_s[source]
            query_grad_place[h, target, :] = query_grad_s[source]
            return 0

        lax.fori_loop(0, GROUP_BLOCKS, put_head, 0)

        out_at = pl.ds(pl.multiple_of(own_columns + h * HEAD_SIZE, HEAD_SIZE), HEAD_SIZE)
        for index, (source, target) in enumerate(
            ((attn_place, attn_out), (query_grad_place, query_grad_out))
        ):
            for step, peer in enumerate(out_peers):
                copy = copy_to(
                    source.at[h, taken(peer), :],
                    target.at[:, out_at],
                    out_send.at[h, index, step],
                    out_recv.at[h, index, step],
                    out_device[step],
                )
                copy.start()
                sent.append(copy)
            keep = pltpu.make_async_copy(
                source.at[h, taken(lane), :], target.at[:, out_at], out_local.at[2 * h + index]
            )
            keep.start()
            stores.append(keep)

    def put_pair(place, _):
        source, target = place_at[place], to_slot(place)
        pair_place[0, target, :] = (key_total[source] * scale).astype(jnp.bfloat16)
        pair_place[1, target, :] = value_total[source].astype(jnp.bfloat16)
        return 0

    lax.fori_loop(0, GROUP_BLOCKS, put_pair, 0)
    swap = copy_to(pair_place.at[1 - kind], other, swap_sems.at[0], swap_sems.at[1], sibling)
    swap.start()
    swap.wait()

    def add_pair(place, _):
        at = to_slot(place)
        total = pair_place[kind, at, :].astype(jnp.float32) + other[at, :].astype(jnp.float32)
        mine[at, :] = total.astype(jnp.bfloat16)
        return 0

    lax.fori_loop(0, GROUP_BLOCKS, add_pair, 0)
    pair_at = pl.ds(pl.multiple_of(lane // sharers * HEAD_SIZE, HEAD_SIZE), HEAD_SIZE)
    pair_landing = pair_out.at[kind, lane % sharers // 2, :, pair_at]
    keep = pltpu.make_async_copy(mine.at[taken(lane), :], pair_landing, out_local.at[2 * heads])
    keep.start()
    stores.append(keep)
    for step, peer in enumerate(out_peers):
        copy = copy_to(
            mine.at[taken(peer), :],
            pair_landing,
            part_send.at[step],
            part_recv.at[step],
            out_device[step],
        )
        copy.start()
        sent.append(copy)
    for keep in stores:
        keep.wait()
    for pair in pairs:
        pair.wait_send()
    for copies in head_copies:
        for copy in copies:
            copy.wait_send()
    for copy in sent:
        copy.wait()


def fused(head_dim, query, grad, key, value, doc_blocks, block_perm):
    rows, width = query.shape
    unit = math.gcd(rows, MASK_BLOCK_SIZE)
    members = GROUP_DEV * head_dim
    wide = width // members
    heads = wide // HEAD_SIZE
    sharers = RATIO // heads
    tokens = rows * members
    out_rows = tokens // GROUP_DEV
    any_spec = pl.BlockSpec(memory_space=pl.ANY)
    smem = pl.BlockSpec(memory_space=pltpu.SMEM)

    def low(*shape):
        return pltpu.VMEM(shape, jnp.bfloat16)

    def full(*shape):
        return pltpu.VMEM(shape, jnp.float32)

    dma = pltpu.SemaphoreType.DMA
    flat, turned = (tokens, HEAD_SIZE), (HEAD_SIZE, tokens)
    landed = (tokens // unit, unit, HEAD_SIZE)
    blocked = (tokens // MASK_BLOCK_SIZE, MASK_BLOCK_SIZE, HEAD_SIZE)
    query, grad, key, value = (
        pltpu.with_memory_space_constraint(array.reshape(rows // unit, unit, -1), pltpu.HBM)
        for array in (query, grad, key, value)
    )
    doc_blocks, block_perm = (
        pltpu.with_memory_space_constraint(array, pltpu.HBM) for array in (doc_blocks, block_perm)
    )
    return pl.pallas_call(
        partial(fused_kernel, head_dim, heads),
        out_shape=[
            jax.ShapeDtypeStruct((out_rows, wide * GROUP_DEV), jnp.bfloat16),
            jax.ShapeDtypeStruct((out_rows, wide * GROUP_DEV), jnp.bfloat16),
            jax.ShapeDtypeStruct(
                (2, sharers // 2, out_rows, HEAD_SIZE * GROUP_DEV // sharers), jnp.bfloat16
            ),
        ],
        in_specs=[smem, smem] + [any_spec] * 4,
        out_specs=[any_spec] * 3,
        scratch_shapes=[low(*landed) for _ in range(2 * heads)]
        + [low(2, *landed)]
        + [low(*flat), low(*flat), low(*turned), low(*turned)] * 2
        + [full(LONG_TOKENS, CHUNK), full(HEAD_SIZE, CHUNK), full(HEAD_SIZE, CHUNK)]
        + [full(*blocked), full(*blocked), low(*blocked), low(*blocked)]
        + [low(heads, *flat), low(heads, *flat), low(2, *flat), low(*flat), low(*flat)]
        + [pltpu.SMEM((GROUP_BLOCKS,), jnp.int32)] * 3
        + [dma((heads, 2, members - 1))] * 2
        + [dma((members - 1,))] * 2
        + [dma((members,))] * 2
        + [dma((heads, 2, GROUP_DEV - 1))] * 2
        + [dma((GROUP_DEV - 1,))] * 2
        + [dma((2,)), dma((2 * heads + 1,)), dma((2 * heads + 1,))],
        compiler_params=pltpu.CompilerParams(
            collective_id=0, has_side_effects=True, vmem_limit_bytes=40 * 1024 * 1024
        ),
        name="fused",
    )(doc_blocks, block_perm, query, grad, key, value)


def body(head_dim, query_rows, key_rows, value_rows, grad_rows, doc_blocks, block_perm):
    attn, query_grad, parts = fused(
        head_dim, query_rows, grad_rows, key_rows, value_rows, doc_blocks, block_perm
    )
    if parts.shape[1] > 1:
        parts = jnp.sum(parts.astype(jnp.float32), axis=1).astype(jnp.bfloat16)
    else:
        parts = parts[:, 0]
    return attn, query_grad, parts[0], parts[1]


def solution(mesh):
    split = P(("ctx", "head"), None)
    out_spec = P("ctx", "head")
    return jax.shard_map(
        partial(body, mesh.shape["head"]),
        mesh=mesh,
        in_specs=(split, split, split, split, P(), P()),
        out_specs=(out_spec,) * 4,
        check_vma=False,
    )
```

```python
from functools import partial
import math

import jax
import jax.numpy as jnp
from jax import lax
from jax.experimental import pallas as pl
from jax.experimental.pallas import tpu as pltpu
from jax.sharding import PartitionSpec as P

QUERY_HEADS = 64
KEY_VALUE_HEADS = 8
HEAD_SIZE = 128
MASK_BLOCK_SIZE = 128
GROUP_DEV = 8
GROUP_BLOCKS = 24
MOST = 16

RATIO = QUERY_HEADS // KEY_VALUE_HEADS
MASKED_LOGIT = -1e30
CHUNK = 512
SPAN_TOKENS = GROUP_BLOCKS * MASK_BLOCK_SIZE
LONG_TOKENS = MOST * MASK_BLOCK_SIZE
PIECES = 2
MESH = pl.DeviceIdType.MESH

SPREAD_ORDERS = [
    [13, 4, 8, 15, 6, 10, 5, 12, 9, 7, 14, 11, 1, 3, 2],
    [13, 4, 8, 15, 6, 10, 5, 12, 9, 7, 14, 11, 1, 3, 2],
]
GATHER_ORDERS = [[6, 4, 2, 7, 5, 3, 1], [2, 5, 6, 3, 4, 7, 1]]


def enter(peers):
    barrier = pltpu.get_barrier_semaphore()
    for peer in peers:
        pl.semaphore_signal(barrier, inc=1, device_id=peer, device_id_type=MESH)
    pl.semaphore_wait(barrier, len(peers))


def flipped(index, mask, count):
    result, bit = index, 1
    while bit < count:
        if mask & bit:
            result = result + bit - index // bit % 2 * (2 * bit)
        bit *= 2
    return result


def visiting_order(kind, members):
    order = SPREAD_ORDERS[kind]
    return order if len(order) == members - 1 else list(range(members - 1, 0, -1))


def dot(left, right):
    return jnp.dot(left, right, preferred_element_type=jnp.float32)


def copy_to(source, target, send_sem, recv_sem, device):
    return pltpu.make_async_remote_copy(
        src_ref=source,
        dst_ref=target,
        send_sem=send_sem,
        recv_sem=recv_sem,
        device_id=device,
        device_id_type=MESH,
    )


def fused_kernel(head_dim, heads, *refs):
    refs = list(refs)

    def take(count):
        taken, refs[:] = refs[:count], refs[count:]
        return taken

    docs_ref, perm_ref, query_ref, grad_ref, key_ref, value_ref = take(6)
    attn_out, query_grad_out, pair_out = take(3)
    query_land, grad_land = take(heads), take(heads)
    (pair_land,) = take(1)
    query_s, grad_s, query_t, grad_t, keys, values, keys_t, values_t = take(8)
    store, out_t, query_grad_t, key_total, value_total, out_s, query_grad_s = take(7)
    attn_place, query_grad_place, pair_place, other, mine = take(5)
    slot_at, source_at, place_at = take(3)
    in_send, in_recv, pair_send, pair_recv, pass_send, pass_recv = take(6)
    out_send, out_recv, part_send, part_recv, swap_sems, local_sems, out_local = take(7)

    members = GROUP_DEV * head_dim
    units, unit, _ = query_ref.shape
    wide = heads * HEAD_SIZE
    block = MASK_BLOCK_SIZE
    per_block = block // unit
    per_chunk = CHUNK // block
    out_rows = SPAN_TOKENS // GROUP_DEV
    sharers = RATIO // heads
    scale = HEAD_SIZE ** (-0.5)
    scale_log2 = scale * math.log2(math.e)

    ctx = lax.axis_index("ctx")
    head = lax.axis_index("head")
    group = ctx // GROUP_DEV
    base = group * GROUP_DEV
    lane = ctx - base
    kind = lane % 2
    own = lane * head_dim + head

    def rows_of(member):
        return pl.ds(member * units, units)

    def head_columns(peer_lane, peer_head, h):
        worker = peer_head * GROUP_DEV + peer_lane
        return pl.ds(pl.multiple_of(worker * wide + h * HEAD_SIZE, HEAD_SIZE), HEAD_SIZE)

    def key_columns(peer_lane, peer_head):
        worker = peer_head * GROUP_DEV + peer_lane
        return pl.ds(
            pl.multiple_of(worker * heads // RATIO * HEAD_SIZE, HEAD_SIZE), HEAD_SIZE
        )

    landing = rows_of(own)
    members_at = [flipped(own, mask, members) for mask in range(members)]
    peers = [(member // head_dim, member % head_dim) for member in members_at]
    device = [{"ctx": base + peer_lane, "head": peer_head} for peer_lane, peer_head in peers]
    sibling = {"ctx": base + flipped(lane, 1, GROUP_DEV), "head": head}

    def own_pair(own_kind):
        return pltpu.make_async_copy(
            (key_ref, value_ref)[own_kind].at[:, :, key_columns(lane, head)],
            pair_land.at[own_kind, landing],
            local_sems.at[2 * heads],
        )

    def pair_copy(mask, peer_kind):
        return copy_to(
            (key_ref, value_ref)[peer_kind].at[:, :, key_columns(*peers[mask])],
            pair_land.at[peer_kind, landing],
            pair_send.at[mask - 1],
            pair_recv.at[mask - 1],
            device[mask],
        )

    def head_copy(h, index, mask):
        source, target = ((query_ref, query_land[h]), (grad_ref, grad_land[h]))[index]
        return copy_to(
            source.at[:, :, head_columns(*peers[mask], h)],
            target.at[landing],
            in_send.at[h, index, mask - 1],
            in_recv.at[h, index, mask - 1],
            device[mask],
        )

    loads = []
    for h in range(heads):
        at = head_columns(lane, head, h)
        for index, (source, target) in enumerate(
            ((query_ref, query_land[h]), (grad_ref, grad_land[h]))
        ):
            load = pltpu.make_async_copy(
                source.at[:, :, at], target.at[landing], local_sems.at[2 * h + index]
            )
            load.start()
            loads.append(load)
    for own_kind in range(2):

        @pl.when(kind == own_kind)
        def _(own_kind=own_kind):
            own_pair(own_kind).start()

    enter(device[1:])
    for own_kind in range(2):

        @pl.when(kind == own_kind)
        def _(own_kind=own_kind):
            order = visiting_order(own_kind, members)
            for mask in order:
                pair_copy(mask, (own_kind + mask // head_dim) % 2).start()
            for h in range(heads):
                for mask in order:
                    for index in range(2):
                        head_copy(h, index, mask).start()

    lengths = [docs_ref[group, i] for i in range(docs_ref.shape[1])]
    starts, start = [], jnp.int32(0)
    for length in lengths:
        starts.append(start)
        start = start + length
    big = jnp.int32(0)
    for length, start in zip(lengths, starts):
        big = big + jnp.where(length == MOST, start, 0)
    other_starts = [
        jnp.where(length == MOST, 0, start - jnp.where(start > big, MOST, 0)) * block
        for length, start in zip(lengths, starts)
    ]

    def loader_of(row_block):
        moved = row_block + GROUP_BLOCKS // 2
        return jnp.where(moved >= GROUP_BLOCKS, moved - GROUP_BLOCKS, moved)

    for slot in range(GROUP_BLOCKS):
        if slot < MOST:
            row_block = big + slot
        else:
            other_block = slot - MOST
            row_block = jnp.where(big <= other_block, slot, other_block)
        source_at[slot] = loader_of(row_block)
    for loader in range(GROUP_BLOCKS):
        row_block = (loader + GROUP_BLOCKS // 2) % GROUP_BLOCKS
        slot = row_block - big
        slot = jnp.where(slot >= MOST, row_block, slot)
        slot_at[loader] = jnp.where(slot < 0, row_block + MOST, slot)

    def find(place, _):
        found = jnp.int32(0)
        for loader in range(GROUP_BLOCKS):
            hit = perm_ref[group * GROUP_BLOCKS + loader] == group * GROUP_BLOCKS + place
            found = jnp.where(hit, slot_at[loader], found)
        place_at[place] = found
        return 0

    lax.fori_loop(0, GROUP_BLOCKS, find, 0)

    key_total[...] = jnp.zeros_like(key_total)
    value_total[...] = jnp.zeros_like(value_total)

    def passing(slot, spot):
        copy = copy_to(
            pair_land.at[kind, spot],
            pair_land.at[kind, spot],
            pass_send.at[slot],
            pass_recv.at[slot],
            sibling,
        )
        copy.start()
        return copy

    pltpu.make_async_copy(
        key_ref.at[:, :, key_columns(lane, head)],
        pair_land.at[kind, landing],
        local_sems.at[2 * heads],
    ).wait()
    passes = [passing(members - 1, landing)]
    pairs = []
    for mask in visiting_order(0, members):
        spot = rows_of(members_at[mask])
        pair = copy_to(
            key_ref.at[:, :, key_columns(lane, head)],
            pair_land.at[kind, spot],
            pair_send.at[mask - 1],
            pair_recv.at[mask - 1],
            device[mask],
        )
        pair.wait_recv()
        pairs.append(pair)
        passes.append(passing(mask - 1, spot))
    for copy in passes:
        copy.wait()

    def to_slot(slot):
        return pl.ds(pl.multiple_of(slot * block, block), block)

    def take_pair(slot, _):
        source, target = source_at[slot] * per_block, to_slot(slot)
        for which, flat, turned in ((0, keys, keys_t), (1, values, values_t)):
            rows_in = [pair_land[which, source + part] for part in range(per_block)]
            rows_in = jnp.concatenate(rows_in, axis=0)
            flat[target, :] = rows_in
            turned[:, target] = rows_in.T
        return 0

    lax.fori_loop(0, GROUP_BLOCKS, take_pair, 0)

    token = lax.broadcasted_iota(jnp.int32, (CHUNK, CHUNK), 1)
    key_at = lax.broadcasted_iota(jnp.int32, (CHUNK, CHUNK), 0)

    def tile(first, index, short):
        at = pl.ds(pl.multiple_of(first + index * CHUNK, CHUNK), CHUNK)
        steps = index + 1

        def spot(step):
            return pl.ds(pl.multiple_of(first + step * CHUNK, CHUNK), CHUNK)

        def slot(step):
            return pl.ds(pl.multiple_of(step * CHUNK, CHUNK), CHUNK)

        def blocks(step):
            return pl.ds(first // block + step * per_chunk, per_chunk)

        def blocked(array):
            return array.reshape(per_chunk, block, HEAD_SIZE)

        queries_t = query_t[:, at]
        grads_t = grad_t[:, at]
        column = index * CHUNK + lax.broadcasted_iota(jnp.int32, (1, CHUNK), 1)
        opened = jnp.zeros((1, CHUNK), jnp.int32)
        if short:
            for start in other_starts:
                opened = jnp.maximum(opened, jnp.where(column >= start, start, 0))

        def logits(step, peak, diagonal):
            raw = dot(keys[spot(step), :], queries_t)
            if diagonal:
                allowed = key_at <= token
                if short:
                    allowed = allowed & (key_at >= opened - step * CHUNK)
                raw = jnp.where(allowed, raw, MASKED_LOGIT)
            elif short:
                raw = jnp.where(key_at >= opened - step * CHUNK, raw, MASKED_LOGIT)
            store[slot(step), :] = raw
            return jnp.maximum(peak, jnp.max(raw, axis=0, keepdims=True))

        peak = lax.fori_loop(
            0,
            index,
            lambda step, peak: logits(step, peak, False),
            jnp.full((1, CHUNK), MASKED_LOGIT, jnp.float32),
        )
        peak = logits(index, peak, True) * scale_log2
        out_t[...] = jnp.zeros_like(out_t)

        def mix(step, total):
            mass = jnp.exp2(store[slot(step), :] * scale_log2 - peak)
            store[slot(step), :] = mass
            out_t[...] += dot(values_t[:, spot(step)], mass.astype(jnp.bfloat16))
            return total + jnp.sum(mass, axis=0, keepdims=True)

        total = lax.fori_loop(0, steps, mix, jnp.zeros((1, CHUNK), jnp.float32))
        share = 1.0 / total
        out = (out_t[...] * share).astype(jnp.bfloat16)
        delta = jnp.sum(
            out.astype(jnp.float32) * grads_t.astype(jnp.float32), axis=0, keepdims=True
        )
        out_s[blocks(index)] = blocked(out.T)
        query_grad_t[...] = jnp.zeros_like(query_grad_t)

        def back(step, carry):
            weights = store[slot(step), :] * share
            value_total[blocks(step)] += blocked(dot(weights.astype(jnp.bfloat16), grad_s[at, :]))
            grad_weights = dot(values[spot(step), :], grads_t)
            dlogits = (weights * (grad_weights - delta)).astype(jnp.bfloat16)
            key_total[blocks(step)] += blocked(dot(dlogits, query_s[at, :]))
            query_grad_t[...] += dot(keys_t[:, spot(step)], dlogits)
            return carry

        lax.fori_loop(0, steps, back, 0)
        query_grad_s[blocks(index)] = blocked((query_grad_t[...] * scale).astype(jnp.bfloat16).T)

    own_columns = lane * wide
    out_peers = [flipped(lane, mask, GROUP_DEV) for mask in range(GROUP_DEV)]
    out_device = [{"ctx": base + peer, "head": head} for peer in out_peers]

    def taken(peer):
        return pl.ds(pl.multiple_of(peer * out_rows, 16), out_rows)

    received, sent, stores = [], [], []
    for h in range(heads):
        for load in loads[2 * h : 2 * h + 2]:
            load.wait()
        copies = [head_copy(h, i, mask) for mask in range(1, members) for i in range(2)]
        for copy in copies:
            copy.wait_recv()
        received.extend(copies)

        def take_head(slot, _, h=h):
            source, target = source_at[slot] * per_block, to_slot(slot)
            for land, flat, turned in (
                (query_land[h], query_s, query_t),
                (grad_land[h], grad_s, grad_t),
            ):
                rows_in = [land[source + part] for part in range(per_block)]
                rows_in = jnp.concatenate(rows_in, axis=0)
                flat[target, :] = rows_in
                turned[:, target] = rows_in.T
            return 0

        lax.fori_loop(0, GROUP_BLOCKS, take_head, 0)

        def long_tile(index, _):
            tile(0, index, False)
            return 0

        def short_tile(index, _):
            tile(LONG_TOKENS, index, True)
            return 0

        lax.fori_loop(0, (SPAN_TOKENS - LONG_TOKENS) // CHUNK, short_tile, 0)
        lax.fori_loop(0, LONG_TOKENS // CHUNK, long_tile, 0)

        def put_head(place, _, h=h):
            source, target = place_at[place], to_slot(place)
            attn_place[h, target, :] = out_s[source]
            query_grad_place[h, target, :] = query_grad_s[source]
            return 0

        lax.fori_loop(0, GROUP_BLOCKS, put_head, 0)

        out_at = pl.ds(pl.multiple_of(own_columns + h * HEAD_SIZE, HEAD_SIZE), HEAD_SIZE)

        def out_copy(index, mask, h=h, out_at=out_at):
            source, target = ((attn_place, attn_out), (query_grad_place, query_grad_out))[index]
            return copy_to(
                source.at[h, taken(out_peers[mask]), :],
                target.at[:, out_at],
                out_send.at[h, index, mask - 1],
                out_recv.at[h, index, mask - 1],
                out_device[mask],
            )

        for own_kind in range(2):

            @pl.when(kind == own_kind)
            def _(own_kind=own_kind, out_copy=out_copy):
                for index in range(2):
                    for mask in GATHER_ORDERS[own_kind]:
                        out_copy(index, mask).start()

        sent.extend(out_copy(i, mask) for i in range(2) for mask in range(1, GROUP_DEV))
        for index, (source, target) in enumerate(
            ((attn_place, attn_out), (query_grad_place, query_grad_out))
        ):
            keep = pltpu.make_async_copy(
                source.at[h, taken(lane), :], target.at[:, out_at], out_local.at[2 * h + index]
            )
            keep.start()
            stores.append(keep)

    def put_pair(place, _):
        source, target = place_at[place], to_slot(place)
        pair_place[0, target, :] = (key_total[source] * scale).astype(jnp.bfloat16)
        pair_place[1, target, :] = value_total[source].astype(jnp.bfloat16)
        return 0

    lax.fori_loop(0, GROUP_BLOCKS, put_pair, 0)
    swap = copy_to(pair_place.at[1 - kind], other, swap_sems.at[0], swap_sems.at[1], sibling)
    swap.start()
    swap.wait()

    def add_pair(place, _):
        at = to_slot(place)
        total = pair_place[kind, at, :].astype(jnp.float32) + other[at, :].astype(jnp.float32)
        mine[at, :] = total.astype(jnp.bfloat16)
        return 0

    lax.fori_loop(0, GROUP_BLOCKS, add_pair, 0)
    pair_at = pl.ds(pl.multiple_of(lane // sharers * HEAD_SIZE, HEAD_SIZE), HEAD_SIZE)
    pair_landing = pair_out.at[kind, lane % sharers // 2, :, pair_at]
    keep = pltpu.make_async_copy(mine.at[taken(lane), :], pair_landing, out_local.at[2 * heads])
    keep.start()
    stores.append(keep)
    for mask in GATHER_ORDERS[0]:
        copy = copy_to(
            mine.at[taken(out_peers[mask]), :],
            pair_landing,
            part_send.at[mask - 1],
            part_recv.at[mask - 1],
            out_device[mask],
        )
        copy.start()
        sent.append(copy)
    for keep in stores:
        keep.wait()
    for pair in pairs:
        pair.wait_send()
    for copy in received:
        copy.wait_send()
    for copy in sent:
        copy.wait()


def fused(head_dim, query, grad, key, value, doc_blocks, block_perm):
    rows, width = query.shape
    unit = math.gcd(rows, MASK_BLOCK_SIZE)
    members = GROUP_DEV * head_dim
    wide = width // members
    heads = wide // HEAD_SIZE
    sharers = RATIO // heads
    tokens = rows * members
    out_rows = tokens // GROUP_DEV
    any_spec = pl.BlockSpec(memory_space=pl.ANY)
    smem = pl.BlockSpec(memory_space=pltpu.SMEM)

    def low(*shape):
        return pltpu.VMEM(shape, jnp.bfloat16)

    def full(*shape):
        return pltpu.VMEM(shape, jnp.float32)

    dma = pltpu.SemaphoreType.DMA
    flat, turned = (tokens, HEAD_SIZE), (HEAD_SIZE, tokens)
    landed = (tokens // unit, unit, HEAD_SIZE)
    blocked = (tokens // MASK_BLOCK_SIZE, MASK_BLOCK_SIZE, HEAD_SIZE)
    query, grad, key, value = (
        pltpu.with_memory_space_constraint(array.reshape(rows // unit, unit, -1), pltpu.HBM)
        for array in (query, grad, key, value)
    )
    doc_blocks, block_perm = (
        pltpu.with_memory_space_constraint(array, pltpu.HBM) for array in (doc_blocks, block_perm)
    )
    return pl.pallas_call(
        partial(fused_kernel, head_dim, heads),
        out_shape=[
            jax.ShapeDtypeStruct((out_rows, wide * GROUP_DEV), jnp.bfloat16),
            jax.ShapeDtypeStruct((out_rows, wide * GROUP_DEV), jnp.bfloat16),
            jax.ShapeDtypeStruct(
                (2, sharers // 2, out_rows, HEAD_SIZE * GROUP_DEV // sharers), jnp.bfloat16
            ),
        ],
        in_specs=[smem, smem] + [any_spec] * 4,
        out_specs=[any_spec] * 3,
        scratch_shapes=[low(*landed) for _ in range(2 * heads)]
        + [low(2, *landed)]
        + [low(*flat), low(*flat), low(*turned), low(*turned)] * 2
        + [full(LONG_TOKENS, CHUNK), full(HEAD_SIZE, CHUNK), full(HEAD_SIZE, CHUNK)]
        + [full(*blocked), full(*blocked), low(*blocked), low(*blocked)]
        + [low(heads, *flat), low(heads, *flat), low(2, *flat), low(*flat), low(*flat)]
        + [pltpu.SMEM((GROUP_BLOCKS,), jnp.int32)] * 3
        + [dma((heads, 2, members - 1))] * 2
        + [dma((members - 1,))] * 2
        + [dma((members,))] * 2
        + [dma((heads, 2, GROUP_DEV - 1))] * 2
        + [dma((GROUP_DEV - 1,))] * 2
        + [dma((2,)), dma((2 * heads + 1,)), dma((2 * heads + 1,))],
        compiler_params=pltpu.CompilerParams(
            collective_id=0, has_side_effects=True, vmem_limit_bytes=40 * 1024 * 1024
        ),
        name="fused",
    )(doc_blocks, block_perm, query, grad, key, value)


def keep_kernel(attn_ref, query_ref, parts_ref, attn_out, query_out, key_out, value_out, sems):
    rows = attn_ref.shape[0] // PIECES
    copies = []
    for piece in range(PIECES):
        at = pl.ds(piece * rows, rows)
        for index, (source, target) in enumerate(
            (
                (attn_ref.at[at, :], attn_out.at[at, :]),
                (query_ref.at[at, :], query_out.at[at, :]),
                (parts_ref.at[0, 0, at, :], key_out.at[at, :]),
                (parts_ref.at[1, 0, at, :], value_out.at[at, :]),
            )
        ):
            copies.append(pltpu.make_async_copy(source, target, sems.at[index, piece]))
    for copy in copies:
        copy.start()
    for copy in copies:
        copy.wait()


def keep(attn, query_grad, parts):
    any_spec = pl.BlockSpec(memory_space=pl.ANY)
    part = jax.ShapeDtypeStruct(parts.shape[2:], jnp.bfloat16)
    whole = jax.ShapeDtypeStruct(attn.shape, jnp.bfloat16)
    return pl.pallas_call(
        keep_kernel,
        out_shape=[whole, whole, part, part],
        in_specs=[any_spec] * 3,
        out_specs=[any_spec] * 4,
        scratch_shapes=[pltpu.SemaphoreType.DMA((4, PIECES))],
        compiler_params=pltpu.CompilerParams(vmem_limit_bytes=1024 * 1024),
        name="keep",
    )(attn, query_grad, parts)


def body(head_dim, query_rows, key_rows, value_rows, grad_rows, doc_blocks, block_perm):
    attn, query_grad, parts = fused(
        head_dim, query_rows, grad_rows, key_rows, value_rows, doc_blocks, block_perm
    )
    if parts.shape[1] == 1:
        return keep(attn, query_grad, parts)
    parts = jnp.sum(parts.astype(jnp.float32), axis=1).astype(jnp.bfloat16)
    return attn, query_grad, parts[0], parts[1]


def solution(mesh):
    split = P(("ctx", "head"), None)
    out_spec = P("ctx", "head")
    return jax.shard_map(
        partial(body, mesh.shape["head"]),
        mesh=mesh,
        in_specs=(split, split, split, split, P(), P()),
        out_specs=(out_spec,) * 4,
        check_vma=False,
    )
```

```python
from functools import partial
import math

import jax
import jax.numpy as jnp
from jax import lax
from jax.experimental import pallas as pl
from jax.experimental.pallas import tpu as pltpu
from jax.sharding import PartitionSpec as P

QUERY_HEADS = 64
KEY_VALUE_HEADS = 8
HEAD_SIZE = 128
MASK_BLOCK_SIZE = 128
GROUP_DEV = 8
GROUP_BLOCKS = 24
MOST = 16

RATIO = QUERY_HEADS // KEY_VALUE_HEADS
MASKED_LOGIT = -1e30
CHUNK = 512
SPAN_TOKENS = GROUP_BLOCKS * MASK_BLOCK_SIZE
LONG_TOKENS = MOST * MASK_BLOCK_SIZE
IN_GROUPS = ((0, 1), (1, 1), (2, 2))
OUT_GROUPS = ((0, 2), (2, 1), (3, 1))
PIECES = 2
MESH = pl.DeviceIdType.MESH

SPREAD_ORDERS = [
    [13, 4, 8, 15, 6, 10, 5, 12, 9, 7, 14, 11, 1, 3, 2],
    [13, 4, 8, 15, 6, 10, 5, 12, 9, 7, 14, 11, 1, 3, 2],
]
GATHER_ORDERS = [[6, 4, 2, 7, 5, 3, 1], [2, 5, 6, 3, 4, 7, 1]]


def greet(peers):
    barrier = pltpu.get_barrier_semaphore()
    for peer in peers:
        pl.semaphore_signal(barrier, inc=1, device_id=peer, device_id_type=MESH)


def flipped(index, mask, count):
    result, bit = index, 1
    while bit < count:
        if mask & bit:
            result = result + bit - index // bit % 2 * (2 * bit)
        bit *= 2
    return result


def visiting_order(kind, members):
    order = SPREAD_ORDERS[kind]
    return order if len(order) == members - 1 else list(range(members - 1, 0, -1))


def grouped(groups, heads):
    if sum(count for _, count in groups) == heads:
        return groups
    return tuple((h, 1) for h in range(heads))


def dot(left, right):
    return jnp.dot(left, right, preferred_element_type=jnp.float32)


def copy_to(source, target, send_sem, recv_sem, device):
    return pltpu.make_async_remote_copy(
        src_ref=source,
        dst_ref=target,
        send_sem=send_sem,
        recv_sem=recv_sem,
        device_id=device,
        device_id_type=MESH,
    )


def fused_kernel(head_dim, heads, *refs):
    refs = list(refs)

    def take(count):
        taken, refs[:] = refs[:count], refs[count:]
        return taken

    docs_ref, perm_ref, query_ref, grad_ref, key_ref, value_ref = take(6)
    attn_out, query_grad_out, pair_out = take(3)
    in_groups, out_groups = grouped(IN_GROUPS, heads), grouped(OUT_GROUPS, heads)
    query_land, grad_land = take(len(in_groups)), take(len(in_groups))
    (pair_land,) = take(1)
    query_s, grad_s, query_t, grad_t, keys, values, keys_t, values_t = take(8)
    store, out_t, query_grad_t, key_total, value_total, out_s, query_grad_s = take(7)
    attn_place, query_grad_place = take(len(out_groups)), take(len(out_groups))
    pair_place, other, mine = take(3)
    slot_at, source_at, place_at = take(3)
    in_send, in_recv, pair_send, pair_recv, pass_send, pass_recv = take(6)
    out_send, out_recv, part_send, part_recv, swap_sems, local_sems, out_local = take(7)

    members = GROUP_DEV * head_dim
    units, unit, _ = query_ref.shape
    wide = heads * HEAD_SIZE
    block = MASK_BLOCK_SIZE
    per_block = block // unit
    per_chunk = CHUNK // block
    out_rows = SPAN_TOKENS // GROUP_DEV
    sharers = RATIO // heads
    scale = HEAD_SIZE ** (-0.5)
    scale_log2 = scale * math.log2(math.e)

    ctx = lax.axis_index("ctx")
    head = lax.axis_index("head")
    group = ctx // GROUP_DEV
    base = group * GROUP_DEV
    lane = ctx - base
    kind = lane % 2
    own = lane * head_dim + head

    def rows_of(member):
        return pl.ds(member * units, units)

    def head_columns(peer_lane, peer_head, g):
        first, count = in_groups[g]
        start = (peer_head * GROUP_DEV + peer_lane) * wide + first * HEAD_SIZE
        return pl.ds(pl.multiple_of(start, HEAD_SIZE), count * HEAD_SIZE)

    def key_columns(peer_lane, peer_head):
        worker = peer_head * GROUP_DEV + peer_lane
        return pl.ds(
            pl.multiple_of(worker * heads // RATIO * HEAD_SIZE, HEAD_SIZE), HEAD_SIZE
        )

    landing = rows_of(own)
    members_at = [flipped(own, mask, members) for mask in range(members)]
    peers = [(member // head_dim, member % head_dim) for member in members_at]
    device = [{"ctx": base + peer_lane, "head": peer_head} for peer_lane, peer_head in peers]
    sibling = {"ctx": base + flipped(lane, 1, GROUP_DEV), "head": head}

    def own_pair(own_kind):
        return pltpu.make_async_copy(
            (key_ref, value_ref)[own_kind].at[:, :, key_columns(lane, head)],
            pair_land.at[own_kind, landing],
            local_sems.at[2 * heads],
        )

    def pair_copy(mask, peer_kind):
        return copy_to(
            (key_ref, value_ref)[peer_kind].at[:, :, key_columns(*peers[mask])],
            pair_land.at[peer_kind, landing],
            pair_send.at[mask - 1],
            pair_recv.at[mask - 1],
            device[mask],
        )

    def head_copy(h, index, mask):
        source, target = ((query_ref, query_land[h]), (grad_ref, grad_land[h]))[index]
        return copy_to(
            source.at[:, :, head_columns(*peers[mask], h)],
            target.at[landing],
            in_send.at[h, index, mask - 1],
            in_recv.at[h, index, mask - 1],
            device[mask],
        )

    greet(device[1:])
    loads = []
    for h in range(len(in_groups)):
        at = head_columns(lane, head, h)
        for index, (source, target) in enumerate(
            ((query_ref, query_land[h]), (grad_ref, grad_land[h]))
        ):
            load = pltpu.make_async_copy(
                source.at[:, :, at], target.at[landing], local_sems.at[2 * h + index]
            )
            load.start()
            loads.append(load)
    for own_kind in range(2):

        @pl.when(kind == own_kind)
        def _(own_kind=own_kind):
            own_pair(own_kind).start()

    pl.semaphore_wait(pltpu.get_barrier_semaphore(), members - 1)
    for own_kind in range(2):

        @pl.when(kind == own_kind)
        def _(own_kind=own_kind):
            order = visiting_order(own_kind, members)
            for mask in order:
                pair_copy(mask, (own_kind + mask // head_dim) % 2).start()
            for h in range(len(in_groups)):
                for index in range(2):
                    for mask in order:
                        head_copy(h, index, mask).start()

    lengths = [docs_ref[group, i] for i in range(docs_ref.shape[1])]
    starts, start = [], jnp.int32(0)
    for length in lengths:
        starts.append(start)
        start = start + length
    big = jnp.int32(0)
    for length, start in zip(lengths, starts):
        big = big + jnp.where(length == MOST, start, 0)
    other_starts = [
        jnp.where(length == MOST, 0, start - jnp.where(start > big, MOST, 0)) * block
        for length, start in zip(lengths, starts)
    ]

    def loader_of(row_block):
        moved = row_block + GROUP_BLOCKS // 2
        return jnp.where(moved >= GROUP_BLOCKS, moved - GROUP_BLOCKS, moved)

    for slot in range(GROUP_BLOCKS):
        if slot < MOST:
            row_block = big + slot
        else:
            other_block = slot - MOST
            row_block = jnp.where(big <= other_block, slot, other_block)
        source_at[slot] = loader_of(row_block)
    for loader in range(GROUP_BLOCKS):
        row_block = (loader + GROUP_BLOCKS // 2) % GROUP_BLOCKS
        slot = row_block - big
        slot = jnp.where(slot >= MOST, row_block, slot)
        slot_at[loader] = jnp.where(slot < 0, row_block + MOST, slot)

    def find(place, _):
        found = jnp.int32(0)
        for loader in range(GROUP_BLOCKS):
            hit = perm_ref[group * GROUP_BLOCKS + loader] == group * GROUP_BLOCKS + place
            found = jnp.where(hit, slot_at[loader], found)
        place_at[place] = found
        return 0

    lax.fori_loop(0, GROUP_BLOCKS, find, 0)

    key_total[...] = jnp.zeros_like(key_total)
    value_total[...] = jnp.zeros_like(value_total)

    def passing(slot, spot):
        copy = copy_to(
            pair_land.at[kind, spot],
            pair_land.at[kind, spot],
            pass_send.at[slot],
            pass_recv.at[slot],
            sibling,
        )
        copy.start()
        return copy

    pltpu.make_async_copy(
        key_ref.at[:, :, key_columns(lane, head)],
        pair_land.at[kind, landing],
        local_sems.at[2 * heads],
    ).wait()
    passes = [passing(members - 1, landing)]
    pairs = []
    for mask in visiting_order(0, members):
        spot = rows_of(members_at[mask])
        pair = copy_to(
            key_ref.at[:, :, key_columns(lane, head)],
            pair_land.at[kind, spot],
            pair_send.at[mask - 1],
            pair_recv.at[mask - 1],
            device[mask],
        )
        pair.wait_recv()
        pairs.append(pair)
        passes.append(passing(mask - 1, spot))
    for copy in passes:
        copy.wait()

    def to_slot(slot):
        return pl.ds(pl.multiple_of(slot * block, block), block)

    def take_pair(slot, _):
        source, target = source_at[slot] * per_block, to_slot(slot)
        for which, flat, turned in ((0, keys, keys_t), (1, values, values_t)):
            rows_in = [pair_land[which, source + part] for part in range(per_block)]
            rows_in = jnp.concatenate(rows_in, axis=0)
            flat[target, :] = rows_in
            turned[:, target] = rows_in.T
        return 0

    lax.fori_loop(0, GROUP_BLOCKS, take_pair, 0)

    token = lax.broadcasted_iota(jnp.int32, (CHUNK, CHUNK), 1)
    key_at = lax.broadcasted_iota(jnp.int32, (CHUNK, CHUNK), 0)

    def tile(first, index, short):
        at = pl.ds(pl.multiple_of(first + index * CHUNK, CHUNK), CHUNK)
        steps = index + 1

        def spot(step):
            return pl.ds(pl.multiple_of(first + step * CHUNK, CHUNK), CHUNK)

        def slot(step):
            return pl.ds(pl.multiple_of(step * CHUNK, CHUNK), CHUNK)

        def blocks(step):
            return pl.ds(first // block + step * per_chunk, per_chunk)

        def blocked(array):
            return array.reshape(per_chunk, block, HEAD_SIZE)

        queries_t = query_t[:, at]
        grads_t = grad_t[:, at]
        column = index * CHUNK + lax.broadcasted_iota(jnp.int32, (1, CHUNK), 1)
        opened = jnp.zeros((1, CHUNK), jnp.int32)
        if short:
            for start in other_starts:
                opened = jnp.maximum(opened, jnp.where(column >= start, start, 0))

        def logits(step, peak, diagonal):
            raw = dot(keys[spot(step), :], queries_t)
            if diagonal:
                allowed = key_at <= token
                if short:
                    allowed = allowed & (key_at >= opened - step * CHUNK)
                raw = jnp.where(allowed, raw, MASKED_LOGIT)
            elif short:
                raw = jnp.where(key_at >= opened - step * CHUNK, raw, MASKED_LOGIT)
            store[slot(step), :] = raw
            return jnp.maximum(peak, jnp.max(raw, axis=0, keepdims=True))

        peak = lax.fori_loop(
            0,
            index,
            lambda step, peak: logits(step, peak, False),
            jnp.full((1, CHUNK), MASKED_LOGIT, jnp.float32),
        )
        peak = logits(index, peak, True) * scale_log2
        out_t[...] = jnp.zeros_like(out_t)

        def mix(step, total):
            mass = jnp.exp2(store[slot(step), :] * scale_log2 - peak)
            store[slot(step), :] = mass
            out_t[...] += dot(values_t[:, spot(step)], mass.astype(jnp.bfloat16))
            return total + jnp.sum(mass, axis=0, keepdims=True)

        total = lax.fori_loop(0, steps, mix, jnp.zeros((1, CHUNK), jnp.float32))
        share = 1.0 / total
        out = (out_t[...] * share).astype(jnp.bfloat16)
        delta = jnp.sum(
            out.astype(jnp.float32) * grads_t.astype(jnp.float32), axis=0, keepdims=True
        )
        out_s[blocks(index)] = blocked(out.T)
        query_grad_t[...] = jnp.zeros_like(query_grad_t)

        def back(step, carry):
            weights = store[slot(step), :] * share
            value_total[blocks(step)] += blocked(dot(weights.astype(jnp.bfloat16), grad_s[at, :]))
            grad_weights = dot(values[spot(step), :], grads_t)
            dlogits = (weights * (grad_weights - delta)).astype(jnp.bfloat16)
            key_total[blocks(step)] += blocked(dot(dlogits, query_s[at, :]))
            query_grad_t[...] += dot(keys_t[:, spot(step)], dlogits)
            return carry

        lax.fori_loop(0, steps, back, 0)
        query_grad_s[blocks(index)] = blocked((query_grad_t[...] * scale).astype(jnp.bfloat16).T)

    own_columns = lane * wide
    out_peers = [flipped(lane, mask, GROUP_DEV) for mask in range(GROUP_DEV)]
    out_device = [{"ctx": base + peer, "head": head} for peer in out_peers]

    def taken(peer):
        return pl.ds(pl.multiple_of(peer * out_rows, 16), out_rows)

    received, sent, stores = [], [], []
    for h in range(heads):
        g, column = [(g, h - first) for g, (first, n) in enumerate(in_groups) if first <= h < first + n][0]
        column = slice(column * HEAD_SIZE, (column + 1) * HEAD_SIZE)
        if column.start == 0:
            for load in loads[2 * g : 2 * g + 2]:
                load.wait()
            copies = [head_copy(g, i, mask) for mask in range(1, members) for i in range(2)]
            for copy in copies:
                copy.wait_recv()
            received.extend(copies)

        def take_head(slot, _, g=g, column=column):
            source, target = source_at[slot] * per_block, to_slot(slot)
            for land, flat, turned in (
                (query_land[g], query_s, query_t),
                (grad_land[g], grad_s, grad_t),
            ):
                rows_in = [land[source + part][:, column] for part in range(per_block)]
                rows_in = jnp.concatenate(rows_in, axis=0)
                flat[target, :] = rows_in
                turned[:, target] = rows_in.T
            return 0

        lax.fori_loop(0, GROUP_BLOCKS, take_head, 0)

        def long_tile(index, _):
            tile(0, index, False)
            return 0

        def short_tile(index, _):
            tile(LONG_TOKENS, index, True)
            return 0

        lax.fori_loop(0, (SPAN_TOKENS - LONG_TOKENS) // CHUNK, short_tile, 0)
        lax.fori_loop(0, LONG_TOKENS // CHUNK, long_tile, 0)

        o, out_column = [(g, h - first) for g, (first, n) in enumerate(out_groups) if first <= h < first + n][0]
        first, count = out_groups[o]
        column = slice(out_column * HEAD_SIZE, (out_column + 1) * HEAD_SIZE)

        def put_head(place, _, o=o, column=column):
            source, target = place_at[place], to_slot(place)
            attn_place[o][target, column] = out_s[source]
            query_grad_place[o][target, column] = query_grad_s[source]
            return 0

        lax.fori_loop(0, GROUP_BLOCKS, put_head, 0)

        if h + 1 < first + count:
            continue
        out_at = own_columns + first * HEAD_SIZE
        out_at = pl.ds(pl.multiple_of(out_at, HEAD_SIZE), count * HEAD_SIZE)

        def out_copy(index, mask, o=o, out_at=out_at):
            source, target = ((attn_place, attn_out), (query_grad_place, query_grad_out))[index]
            return copy_to(
                source[o].at[taken(out_peers[mask]), :],
                target.at[:, out_at],
                out_send.at[o, index, mask - 1],
                out_recv.at[o, index, mask - 1],
                out_device[mask],
            )

        for own_kind in range(2):

            @pl.when(kind == own_kind)
            def _(own_kind=own_kind, out_copy=out_copy):
                for index in range(2):
                    for mask in GATHER_ORDERS[own_kind]:
                        out_copy(index, mask).start()

        sent.extend(out_copy(i, mask) for i in range(2) for mask in range(1, GROUP_DEV))
        for index, (source, target) in enumerate(
            ((attn_place, attn_out), (query_grad_place, query_grad_out))
        ):
            keep = pltpu.make_async_copy(
                source[o].at[taken(lane), :], target.at[:, out_at], out_local.at[2 * o + index]
            )
            keep.start()
            stores.append(keep)

    def put_pair(place, _):
        source, target = place_at[place], to_slot(place)
        pair_place[0, target, :] = (key_total[source] * scale).astype(jnp.bfloat16)
        pair_place[1, target, :] = value_total[source].astype(jnp.bfloat16)
        return 0

    lax.fori_loop(0, GROUP_BLOCKS, put_pair, 0)
    swap = copy_to(pair_place.at[1 - kind], other, swap_sems.at[0], swap_sems.at[1], sibling)
    swap.start()
    swap.wait()

    def add_pair(place, _):
        at = to_slot(place)
        total = pair_place[kind, at, :].astype(jnp.float32) + other[at, :].astype(jnp.float32)
        mine[at, :] = total.astype(jnp.bfloat16)
        return 0

    lax.fori_loop(0, GROUP_BLOCKS, add_pair, 0)
    pair_at = pl.ds(pl.multiple_of(lane // sharers * HEAD_SIZE, HEAD_SIZE), HEAD_SIZE)
    pair_landing = pair_out.at[kind, lane % sharers // 2, :, pair_at]
    keep = pltpu.make_async_copy(mine.at[taken(lane), :], pair_landing, out_local.at[2 * heads])
    keep.start()
    stores.append(keep)
    for mask in GATHER_ORDERS[0]:
        copy = copy_to(
            mine.at[taken(out_peers[mask]), :],
            pair_landing,
            part_send.at[mask - 1],
            part_recv.at[mask - 1],
            out_device[mask],
        )
        copy.start()
        sent.append(copy)
    for keep in stores:
        keep.wait()
    for pair in pairs:
        pair.wait_send()
    for copy in received:
        copy.wait_send()
    for copy in sent:
        copy.wait()


def fused(head_dim, query, grad, key, value, doc_blocks, block_perm):
    rows, width = query.shape
    unit = math.gcd(rows, MASK_BLOCK_SIZE)
    members = GROUP_DEV * head_dim
    wide = width // members
    heads = wide // HEAD_SIZE
    sharers = RATIO // heads
    tokens = rows * members
    out_rows = tokens // GROUP_DEV
    any_spec = pl.BlockSpec(memory_space=pl.ANY)
    smem = pl.BlockSpec(memory_space=pltpu.SMEM)

    def low(*shape):
        return pltpu.VMEM(shape, jnp.bfloat16)

    def full(*shape):
        return pltpu.VMEM(shape, jnp.float32)

    dma = pltpu.SemaphoreType.DMA
    in_groups, out_groups = grouped(IN_GROUPS, heads), grouped(OUT_GROUPS, heads)
    flat, turned = (tokens, HEAD_SIZE), (HEAD_SIZE, tokens)
    landed = (tokens // unit, unit, HEAD_SIZE)
    blocked = (tokens // MASK_BLOCK_SIZE, MASK_BLOCK_SIZE, HEAD_SIZE)
    query, grad, key, value = (
        pltpu.with_memory_space_constraint(array.reshape(rows // unit, unit, -1), pltpu.HBM)
        for array in (query, grad, key, value)
    )
    doc_blocks, block_perm = (
        pltpu.with_memory_space_constraint(array, pltpu.HBM) for array in (doc_blocks, block_perm)
    )
    return pl.pallas_call(
        partial(fused_kernel, head_dim, heads),
        out_shape=[
            jax.ShapeDtypeStruct((out_rows, wide * GROUP_DEV), jnp.bfloat16),
            jax.ShapeDtypeStruct((out_rows, wide * GROUP_DEV), jnp.bfloat16),
            jax.ShapeDtypeStruct(
                (2, sharers // 2, out_rows, HEAD_SIZE * GROUP_DEV // sharers), jnp.bfloat16
            ),
        ],
        in_specs=[smem, smem] + [any_spec] * 4,
        out_specs=[any_spec] * 3,
        scratch_shapes=[low(*landed[:2], n * HEAD_SIZE) for _, n in in_groups * 2]
        + [low(2, *landed)]
        + [low(*flat), low(*flat), low(*turned), low(*turned)] * 2
        + [full(LONG_TOKENS, CHUNK), full(HEAD_SIZE, CHUNK), full(HEAD_SIZE, CHUNK)]
        + [full(*blocked), full(*blocked), low(*blocked), low(*blocked)]
        + [low(tokens, n * HEAD_SIZE) for _, n in out_groups * 2]
        + [low(2, *flat), low(*flat), low(*flat)]
        + [pltpu.SMEM((GROUP_BLOCKS,), jnp.int32)] * 3
        + [dma((heads, 2, members - 1))] * 2
        + [dma((members - 1,))] * 2
        + [dma((members,))] * 2
        + [dma((heads, 2, GROUP_DEV - 1))] * 2
        + [dma((GROUP_DEV - 1,))] * 2
        + [dma((2,)), dma((2 * heads + 1,)), dma((2 * heads + 1,))],
        compiler_params=pltpu.CompilerParams(
            collective_id=0, has_side_effects=True, vmem_limit_bytes=40 * 1024 * 1024
        ),
        name="fused",
    )(doc_blocks, block_perm, query, grad, key, value)


def keep_kernel(attn_ref, query_ref, parts_ref, attn_out, query_out, key_out, value_out, sems):
    rows = attn_ref.shape[0] // PIECES
    copies = []
    for piece in range(PIECES):
        at = pl.ds(piece * rows, rows)
        for index, (source, target) in enumerate(
            (
                (attn_ref.at[at, :], attn_out.at[at, :]),
                (query_ref.at[at, :], query_out.at[at, :]),
                (parts_ref.at[0, 0, at, :], key_out.at[at, :]),
                (parts_ref.at[1, 0, at, :], value_out.at[at, :]),
            )
        ):
            copies.append(pltpu.make_async_copy(source, target, sems.at[index, piece]))
    for copy in copies:
        copy.start()
    for copy in copies:
        copy.wait()


def keep(attn, query_grad, parts):
    any_spec = pl.BlockSpec(memory_space=pl.ANY)
    part = jax.ShapeDtypeStruct(parts.shape[2:], jnp.bfloat16)
    whole = jax.ShapeDtypeStruct(attn.shape, jnp.bfloat16)
    return pl.pallas_call(
        keep_kernel,
        out_shape=[whole, whole, part, part],
        in_specs=[any_spec] * 3,
        out_specs=[any_spec] * 4,
        scratch_shapes=[pltpu.SemaphoreType.DMA((4, PIECES))],
        compiler_params=pltpu.CompilerParams(vmem_limit_bytes=1024 * 1024),
        name="keep",
    )(attn, query_grad, parts)


def body(head_dim, query_rows, key_rows, value_rows, grad_rows, doc_blocks, block_perm):
    attn, query_grad, parts = fused(
        head_dim, query_rows, grad_rows, key_rows, value_rows, doc_blocks, block_perm
    )
    if parts.shape[1] == 1:
        return keep(attn, query_grad, parts)
    parts = jnp.sum(parts.astype(jnp.float32), axis=1).astype(jnp.bfloat16)
    return attn, query_grad, parts[0], parts[1]


def solution(mesh):
    split = P(("ctx", "head"), None)
    out_spec = P("ctx", "head")
    return jax.shard_map(
        partial(body, mesh.shape["head"]),
        mesh=mesh,
        in_specs=(split, split, split, split, P(), P()),
        out_specs=(out_spec,) * 4,
        check_vma=False,
    )
```

```python
from functools import partial
import math

import jax
import jax.numpy as jnp
from jax import lax
from jax.experimental import pallas as pl
from jax.experimental.pallas import tpu as pltpu
from jax.sharding import PartitionSpec as P

QUERY_HEADS = 64
KEY_VALUE_HEADS = 8
HEAD_SIZE = 128
MASK_BLOCK_SIZE = 128
GROUP_DEV = 8
GROUP_BLOCKS = 24
MOST = 16

RATIO = QUERY_HEADS // KEY_VALUE_HEADS
MASKED_LOGIT = -1e30
CHUNK = 512
SPAN_TOKENS = GROUP_BLOCKS * MASK_BLOCK_SIZE
LONG_TOKENS = MOST * MASK_BLOCK_SIZE
IN_GROUPS = ((0, 1), (1, 1), (2, 2))
OUT_GROUPS = ((0, 2), (2, 1), (3, 1))
PIECES = 2
MESH = pl.DeviceIdType.MESH

SPREAD_ORDERS = [
    [13, 4, 8, 15, 6, 10, 5, 12, 9, 7, 14, 11, 1, 3, 2],
    [13, 4, 8, 15, 6, 10, 5, 12, 9, 7, 14, 11, 1, 3, 2],
]
GATHER_ORDERS = [[6, 4, 2, 7, 5, 3, 1], [2, 5, 6, 3, 4, 7, 1]]


def greet(peers):
    barrier = pltpu.get_barrier_semaphore()
    for peer in peers:
        pl.semaphore_signal(barrier, inc=1, device_id=peer, device_id_type=MESH)


def flipped(index, mask, count):
    result, bit = index, 1
    while bit < count:
        if mask & bit:
            result = result + bit - index // bit % 2 * (2 * bit)
        bit *= 2
    return result


def visiting_order(kind, members):
    order = SPREAD_ORDERS[kind]
    return order if len(order) == members - 1 else list(range(members - 1, 0, -1))


def grouped(groups, heads):
    if sum(count for _, count in groups) == heads:
        return groups
    return tuple((h, 1) for h in range(heads))


def dot(left, right):
    return jnp.dot(left, right, preferred_element_type=jnp.float32)


def copy_to(source, target, send_sem, recv_sem, device):
    return pltpu.make_async_remote_copy(
        src_ref=source,
        dst_ref=target,
        send_sem=send_sem,
        recv_sem=recv_sem,
        device_id=device,
        device_id_type=MESH,
    )


def fused_kernel(head_dim, heads, *refs):
    refs = list(refs)

    def take(count):
        taken, refs[:] = refs[:count], refs[count:]
        return taken

    docs_ref, perm_ref, query_ref, grad_ref, key_ref, value_ref = take(6)
    attn_out, query_grad_out, pair_out = take(3)
    in_groups, out_groups = grouped(IN_GROUPS, heads), grouped(OUT_GROUPS, heads)
    query_land, grad_land = take(len(in_groups)), take(len(in_groups))
    (pair_land,) = take(1)
    query_s, grad_s, query_t, grad_t, keys, values, keys_t, values_t = take(8)
    store, out_t, query_grad_t, key_total, value_total, out_s, query_grad_s = take(7)
    attn_place, query_grad_place = take(len(out_groups)), take(len(out_groups))
    pair_place, other, mine = take(3)
    slot_at, source_at, place_at = take(3)
    in_send, in_recv, pair_send, pair_recv, pass_send, pass_recv = take(6)
    out_send, out_recv, part_send, part_recv, swap_sems, local_sems, out_local = take(7)

    members = GROUP_DEV * head_dim
    units, unit, _ = query_ref.shape
    wide = heads * HEAD_SIZE
    block = MASK_BLOCK_SIZE
    per_block = block // unit
    per_chunk = CHUNK // block
    out_rows = SPAN_TOKENS // GROUP_DEV
    sharers = RATIO // heads
    scale = HEAD_SIZE ** (-0.5)
    scale_log2 = scale * math.log2(math.e)

    ctx = lax.axis_index("ctx")
    head = lax.axis_index("head")
    group = ctx // GROUP_DEV
    base = group * GROUP_DEV
    lane = ctx - base
    kind = lane % 2
    own = lane * head_dim + head

    def rows_of(member):
        return pl.ds(member * units, units)

    def head_columns(peer_lane, peer_head, g):
        first, count = in_groups[g]
        start = (peer_head * GROUP_DEV + peer_lane) * wide + first * HEAD_SIZE
        return pl.ds(pl.multiple_of(start, HEAD_SIZE), count * HEAD_SIZE)

    def key_columns(peer_lane, peer_head):
        worker = peer_head * GROUP_DEV + peer_lane
        return pl.ds(
            pl.multiple_of(worker * heads // RATIO * HEAD_SIZE, HEAD_SIZE), HEAD_SIZE
        )

    landing = rows_of(own)
    members_at = [flipped(own, mask, members) for mask in range(members)]
    peers = [(member // head_dim, member % head_dim) for member in members_at]
    device = [{"ctx": base + peer_lane, "head": peer_head} for peer_lane, peer_head in peers]
    sibling = {"ctx": base + flipped(lane, 1, GROUP_DEV), "head": head}

    def own_pair(own_kind):
        return pltpu.make_async_copy(
            (key_ref, value_ref)[own_kind].at[:, :, key_columns(lane, head)],
            pair_land.at[own_kind, landing],
            local_sems.at[2 * heads],
        )

    def pair_copy(mask, peer_kind):
        return copy_to(
            (key_ref, value_ref)[peer_kind].at[:, :, key_columns(*peers[mask])],
            pair_land.at[peer_kind, landing],
            pair_send.at[mask - 1],
            pair_recv.at[mask - 1],
            device[mask],
        )

    def head_copy(h, index, mask):
        source, target = ((query_ref, query_land[h]), (grad_ref, grad_land[h]))[index]
        return copy_to(
            source.at[:, :, head_columns(*peers[mask], h)],
            target.at[landing],
            in_send.at[h, index, mask - 1],
            in_recv.at[h, index, mask - 1],
            device[mask],
        )

    greet(device[1:])
    loads = []
    for h in range(len(in_groups)):
        at = head_columns(lane, head, h)
        for index, (source, target) in enumerate(
            ((query_ref, query_land[h]), (grad_ref, grad_land[h]))
        ):
            load = pltpu.make_async_copy(
                source.at[:, :, at], target.at[landing], local_sems.at[2 * h + index]
            )
            load.start()
            loads.append(load)
    for own_kind in range(2):

        @pl.when(kind == own_kind)
        def _(own_kind=own_kind):
            own_pair(own_kind).start()

    pl.semaphore_wait(pltpu.get_barrier_semaphore(), members - 1)
    for own_kind in range(2):

        @pl.when(kind == own_kind)
        def _(own_kind=own_kind):
            order = visiting_order(own_kind, members)
            for mask in order:
                pair_copy(mask, (own_kind + mask // head_dim) % 2).start()
            for h in range(len(in_groups)):
                for index in range(2):
                    for mask in order:
                        head_copy(h, index, mask).start()

    lengths = [docs_ref[group, i] for i in range(docs_ref.shape[1])]
    starts, start = [], jnp.int32(0)
    for length in lengths:
        starts.append(start)
        start = start + length
    big = jnp.int32(0)
    for length, start in zip(lengths, starts):
        big = big + jnp.where(length == MOST, start, 0)
    other_starts = [
        jnp.where(length == MOST, 0, start - jnp.where(start > big, MOST, 0)) * block
        for length, start in zip(lengths, starts)
    ]

    def loader_of(row_block):
        moved = row_block + GROUP_BLOCKS // 2
        return jnp.where(moved >= GROUP_BLOCKS, moved - GROUP_BLOCKS, moved)

    for slot in range(GROUP_BLOCKS):
        if slot < MOST:
            row_block = big + slot
        else:
            other_block = slot - MOST
            row_block = jnp.where(big <= other_block, slot, other_block)
        source_at[slot] = loader_of(row_block)
    for loader in range(GROUP_BLOCKS):
        row_block = (loader + GROUP_BLOCKS // 2) % GROUP_BLOCKS
        slot = row_block - big
        slot = jnp.where(slot >= MOST, row_block, slot)
        slot_at[loader] = jnp.where(slot < 0, row_block + MOST, slot)

    def find(place, _):
        found = jnp.int32(0)
        for loader in range(GROUP_BLOCKS):
            hit = perm_ref[group * GROUP_BLOCKS + loader] == group * GROUP_BLOCKS + place
            found = jnp.where(hit, slot_at[loader], found)
        place_at[place] = found
        return 0

    lax.fori_loop(0, GROUP_BLOCKS, find, 0)

    key_total[...] = jnp.zeros_like(key_total)
    value_total[...] = jnp.zeros_like(value_total)

    def passing(slot, spot):
        copy = copy_to(
            pair_land.at[kind, spot],
            pair_land.at[kind, spot],
            pass_send.at[slot],
            pass_recv.at[slot],
            sibling,
        )
        copy.start()
        return copy

    pltpu.make_async_copy(
        key_ref.at[:, :, key_columns(lane, head)],
        pair_land.at[kind, landing],
        local_sems.at[2 * heads],
    ).wait()
    passes = [passing(members - 1, landing)]
    pairs = []
    for mask in visiting_order(0, members):
        spot = rows_of(members_at[mask])
        pair = copy_to(
            key_ref.at[:, :, key_columns(lane, head)],
            pair_land.at[kind, spot],
            pair_send.at[mask - 1],
            pair_recv.at[mask - 1],
            device[mask],
        )
        pair.wait_recv()
        pairs.append(pair)
        passes.append(passing(mask - 1, spot))
    for copy in passes:
        copy.wait()

    def to_slot(slot):
        return pl.ds(pl.multiple_of(slot * block, block), block)

    def take_pair(slot, _):
        source, target = source_at[slot] * per_block, to_slot(slot)
        for which, flat, turned in ((0, keys, keys_t), (1, values, values_t)):
            rows_in = [pair_land[which, source + part] for part in range(per_block)]
            rows_in = jnp.concatenate(rows_in, axis=0)
            flat[target, :] = rows_in
            turned[:, target] = rows_in.T
        return 0

    lax.fori_loop(0, GROUP_BLOCKS, take_pair, 0)

    token = lax.broadcasted_iota(jnp.int32, (CHUNK, CHUNK), 1)
    key_at = lax.broadcasted_iota(jnp.int32, (CHUNK, CHUNK), 0)

    def tile(first, index, short):
        at = pl.ds(pl.multiple_of(first + index * CHUNK, CHUNK), CHUNK)
        half = CHUNK // 2

        def part(step, low, size):
            start = step * CHUNK + low
            spot = pl.ds(pl.multiple_of(first + start, half), size)
            slot = pl.ds(pl.multiple_of(start, half), size)
            return spot, slot, pl.ds((first + start) // block, size // block)

        def blocks(step):
            return pl.ds(first // block + step * per_chunk, per_chunk)

        def blocked(array):
            return array.reshape(array.shape[0] // block, block, HEAD_SIZE)

        corner = pl.ds(pl.multiple_of(first + index * CHUNK + half, half), half)
        pieces = ((0, half, at, slice(0, CHUNK)), (half, half, corner, slice(half, CHUNK)))

        def joined(left, right):
            return jnp.concatenate([left[:, :half], right], axis=1)

        queries_t = query_t[:, at]
        grads_t = grad_t[:, at]
        column = index * CHUNK + lax.broadcasted_iota(jnp.int32, (1, CHUNK), 1)
        opened = jnp.zeros((1, CHUNK), jnp.int32)
        if short:
            for start in other_starts:
                opened = jnp.maximum(opened, jnp.where(column >= start, start, 0))

        def logits(step, peak, low, size, columns, diagonal):
            spot, slot, _ = part(step, low, size)
            raw = dot(keys[spot, :], queries_t[:, columns])
            keys_at = key_at[:size, columns] + low
            if diagonal:
                allowed = keys_at <= token[:size, columns]
                if short:
                    allowed = allowed & (keys_at >= opened[:, columns] - step * CHUNK)
                raw = jnp.where(allowed, raw, MASKED_LOGIT)
            elif short:
                raw = jnp.where(keys_at >= opened - step * CHUNK, raw, MASKED_LOGIT)
            store[slot, columns] = raw
            return jnp.maximum(peak[:, columns], jnp.max(raw, axis=0, keepdims=True))

        everything = slice(0, CHUNK)
        peak = lax.fori_loop(
            0,
            index,
            lambda step, peak: logits(step, peak, 0, CHUNK, everything, False),
            jnp.full((1, CHUNK), MASKED_LOGIT, jnp.float32),
        )
        peak = logits(index, peak, 0, half, everything, True)
        peak = joined(peak, logits(index, peak, half, half, slice(half, CHUNK), True)) * scale_log2
        out_t[...] = jnp.zeros_like(out_t)

        def mix(step, total, low, size, columns):
            spot, slot, _ = part(step, low, size)
            mass = jnp.exp2(store[slot, columns] * scale_log2 - peak[:, columns])
            store[slot, columns] = mass
            out_t[:, columns] += dot(values_t[:, spot], mass.astype(jnp.bfloat16))
            return total[:, columns] + jnp.sum(mass, axis=0, keepdims=True)

        total = lax.fori_loop(
            0,
            index,
            lambda step, total: mix(step, total, 0, CHUNK, everything),
            jnp.zeros((1, CHUNK), jnp.float32),
        )
        total = mix(index, total, 0, half, everything)
        total = joined(total, mix(index, total, half, half, slice(half, CHUNK)))
        share = 1.0 / total
        out = (out_t[...] * share).astype(jnp.bfloat16)
        delta = jnp.sum(
            out.astype(jnp.float32) * grads_t.astype(jnp.float32), axis=0, keepdims=True
        )
        out_s[blocks(index)] = blocked(out.T)
        query_grad_t[...] = jnp.zeros_like(query_grad_t)

        def back(step, low, size, rows_at, columns):
            spot, slot, spot_blocks = part(step, low, size)
            weights = store[slot, columns] * share[:, columns]
            value_total[spot_blocks] += blocked(dot(weights.astype(jnp.bfloat16), grad_s[rows_at, :]))
            grad_weights = dot(values[spot, :], grads_t[:, columns])
            dlogits = (weights * (grad_weights - delta[:, columns])).astype(jnp.bfloat16)
            key_total[spot_blocks] += blocked(dot(dlogits, query_s[rows_at, :]))
            query_grad_t[:, columns] += dot(keys_t[:, spot], dlogits)

        def back_step(step, carry):
            back(step, 0, CHUNK, at, everything)
            return carry

        lax.fori_loop(0, index, back_step, 0)
        for low, size, rows_at, columns in pieces:
            back(index, low, size, rows_at, columns)
        query_grad_s[blocks(index)] = blocked((query_grad_t[...] * scale).astype(jnp.bfloat16).T)

    own_columns = lane * wide
    out_peers = [flipped(lane, mask, GROUP_DEV) for mask in range(GROUP_DEV)]
    out_device = [{"ctx": base + peer, "head": head} for peer in out_peers]

    def taken(peer):
        return pl.ds(pl.multiple_of(peer * out_rows, 16), out_rows)

    received, sent, stores = [], [], []
    for h in range(heads):
        g, column = [(g, h - first) for g, (first, n) in enumerate(in_groups) if first <= h < first + n][0]
        column = slice(column * HEAD_SIZE, (column + 1) * HEAD_SIZE)
        if column.start == 0:
            for load in loads[2 * g : 2 * g + 2]:
                load.wait()
            copies = [head_copy(g, i, mask) for mask in range(1, members) for i in range(2)]
            for copy in copies:
                copy.wait_recv()
            received.extend(copies)

        def take_head(slot, _, g=g, column=column):
            source, target = source_at[slot] * per_block, to_slot(slot)
            for land, flat, turned in (
                (query_land[g], query_s, query_t),
                (grad_land[g], grad_s, grad_t),
            ):
                rows_in = [land[source + part][:, column] for part in range(per_block)]
                rows_in = jnp.concatenate(rows_in, axis=0)
                flat[target, :] = rows_in
                turned[:, target] = rows_in.T
            return 0

        lax.fori_loop(0, GROUP_BLOCKS, take_head, 0)

        def long_tile(index, _):
            tile(0, index, False)
            return 0

        def short_tile(index, _):
            tile(LONG_TOKENS, index, True)
            return 0

        lax.fori_loop(0, (SPAN_TOKENS - LONG_TOKENS) // CHUNK, short_tile, 0)
        lax.fori_loop(0, LONG_TOKENS // CHUNK, long_tile, 0)

        o, out_column = [(g, h - first) for g, (first, n) in enumerate(out_groups) if first <= h < first + n][0]
        first, count = out_groups[o]
        column = slice(out_column * HEAD_SIZE, (out_column + 1) * HEAD_SIZE)

        def put_head(place, _, o=o, column=column):
            source, target = place_at[place], to_slot(place)
            attn_place[o][target, column] = out_s[source]
            query_grad_place[o][target, column] = query_grad_s[source]
            return 0

        lax.fori_loop(0, GROUP_BLOCKS, put_head, 0)

        if h + 1 < first + count:
            continue
        out_at = own_columns + first * HEAD_SIZE
        out_at = pl.ds(pl.multiple_of(out_at, HEAD_SIZE), count * HEAD_SIZE)

        def out_copy(index, mask, o=o, out_at=out_at):
            source, target = ((attn_place, attn_out), (query_grad_place, query_grad_out))[index]
            return copy_to(
                source[o].at[taken(out_peers[mask]), :],
                target.at[:, out_at],
                out_send.at[o, index, mask - 1],
                out_recv.at[o, index, mask - 1],
                out_device[mask],
            )

        for own_kind in range(2):

            @pl.when(kind == own_kind)
            def _(own_kind=own_kind, out_copy=out_copy):
                for index in range(2):
                    for mask in GATHER_ORDERS[own_kind]:
                        out_copy(index, mask).start()

        sent.extend(out_copy(i, mask) for i in range(2) for mask in range(1, GROUP_DEV))
        for index, (source, target) in enumerate(
            ((attn_place, attn_out), (query_grad_place, query_grad_out))
        ):
            keep = pltpu.make_async_copy(
                source[o].at[taken(lane), :], target.at[:, out_at], out_local.at[2 * o + index]
            )
            keep.start()
            stores.append(keep)

    def put_pair(place, _):
        source, target = place_at[place], to_slot(place)
        pair_place[0, target, :] = (key_total[source] * scale).astype(jnp.bfloat16)
        pair_place[1, target, :] = value_total[source].astype(jnp.bfloat16)
        return 0

    lax.fori_loop(0, GROUP_BLOCKS, put_pair, 0)
    swap = copy_to(pair_place.at[1 - kind], other, swap_sems.at[0], swap_sems.at[1], sibling)
    swap.start()
    swap.wait()

    def add_pair(place, _):
        at = to_slot(place)
        total = pair_place[kind, at, :].astype(jnp.float32) + other[at, :].astype(jnp.float32)
        mine[at, :] = total.astype(jnp.bfloat16)
        return 0

    lax.fori_loop(0, GROUP_BLOCKS, add_pair, 0)
    pair_at = pl.ds(pl.multiple_of(lane // sharers * HEAD_SIZE, HEAD_SIZE), HEAD_SIZE)
    pair_landing = pair_out.at[kind, lane % sharers // 2, :, pair_at]
    keep = pltpu.make_async_copy(mine.at[taken(lane), :], pair_landing, out_local.at[2 * heads])
    keep.start()
    stores.append(keep)
    for mask in GATHER_ORDERS[0]:
        copy = copy_to(
            mine.at[taken(out_peers[mask]), :],
            pair_landing,
            part_send.at[mask - 1],
            part_recv.at[mask - 1],
            out_device[mask],
        )
        copy.start()
        sent.append(copy)
    for keep in stores:
        keep.wait()
    for pair in pairs:
        pair.wait_send()
    for copy in received:
        copy.wait_send()
    for copy in sent:
        copy.wait()


def fused(head_dim, query, grad, key, value, doc_blocks, block_perm):
    rows, width = query.shape
    unit = math.gcd(rows, MASK_BLOCK_SIZE)
    members = GROUP_DEV * head_dim
    wide = width // members
    heads = wide // HEAD_SIZE
    sharers = RATIO // heads
    tokens = rows * members
    out_rows = tokens // GROUP_DEV
    any_spec = pl.BlockSpec(memory_space=pl.ANY)
    smem = pl.BlockSpec(memory_space=pltpu.SMEM)

    def low(*shape):
        return pltpu.VMEM(shape, jnp.bfloat16)

    def full(*shape):
        return pltpu.VMEM(shape, jnp.float32)

    dma = pltpu.SemaphoreType.DMA
    in_groups, out_groups = grouped(IN_GROUPS, heads), grouped(OUT_GROUPS, heads)
    flat, turned = (tokens, HEAD_SIZE), (HEAD_SIZE, tokens)
    landed = (tokens // unit, unit, HEAD_SIZE)
    blocked = (tokens // MASK_BLOCK_SIZE, MASK_BLOCK_SIZE, HEAD_SIZE)
    query, grad, key, value = (
        pltpu.with_memory_space_constraint(array.reshape(rows // unit, unit, -1), pltpu.HBM)
        for array in (query, grad, key, value)
    )
    doc_blocks, block_perm = (
        pltpu.with_memory_space_constraint(array, pltpu.HBM) for array in (doc_blocks, block_perm)
    )
    return pl.pallas_call(
        partial(fused_kernel, head_dim, heads),
        out_shape=[
            jax.ShapeDtypeStruct((out_rows, wide * GROUP_DEV), jnp.bfloat16),
            jax.ShapeDtypeStruct((out_rows, wide * GROUP_DEV), jnp.bfloat16),
            jax.ShapeDtypeStruct(
                (2, sharers // 2, out_rows, HEAD_SIZE * GROUP_DEV // sharers), jnp.bfloat16
            ),
        ],
        in_specs=[smem, smem] + [any_spec] * 4,
        out_specs=[any_spec] * 3,
        scratch_shapes=[low(*landed[:2], n * HEAD_SIZE) for _, n in in_groups * 2]
        + [low(2, *landed)]
        + [low(*flat), low(*flat), low(*turned), low(*turned)] * 2
        + [full(LONG_TOKENS, CHUNK), full(HEAD_SIZE, CHUNK), full(HEAD_SIZE, CHUNK)]
        + [full(*blocked), full(*blocked), low(*blocked), low(*blocked)]
        + [low(tokens, n * HEAD_SIZE) for _, n in out_groups * 2]
        + [low(2, *flat), low(*flat), low(*flat)]
        + [pltpu.SMEM((GROUP_BLOCKS,), jnp.int32)] * 3
        + [dma((heads, 2, members - 1))] * 2
        + [dma((members - 1,))] * 2
        + [dma((members,))] * 2
        + [dma((heads, 2, GROUP_DEV - 1))] * 2
        + [dma((GROUP_DEV - 1,))] * 2
        + [dma((2,)), dma((2 * heads + 1,)), dma((2 * heads + 1,))],
        compiler_params=pltpu.CompilerParams(
            collective_id=0, has_side_effects=True, vmem_limit_bytes=40 * 1024 * 1024
        ),
        name="fused",
    )(doc_blocks, block_perm, query, grad, key, value)


def keep_kernel(attn_ref, query_ref, parts_ref, attn_out, query_out, key_out, value_out, sems):
    rows = attn_ref.shape[0] // PIECES
    copies = []
    for piece in range(PIECES):
        at = pl.ds(piece * rows, rows)
        for index, (source, target) in enumerate(
            (
                (attn_ref.at[at, :], attn_out.at[at, :]),
                (query_ref.at[at, :], query_out.at[at, :]),
                (parts_ref.at[0, 0, at, :], key_out.at[at, :]),
                (parts_ref.at[1, 0, at, :], value_out.at[at, :]),
            )
        ):
            copies.append(pltpu.make_async_copy(source, target, sems.at[index, piece]))
    for copy in copies:
        copy.start()
    for copy in copies:
        copy.wait()


def keep(attn, query_grad, parts):
    any_spec = pl.BlockSpec(memory_space=pl.ANY)
    part = jax.ShapeDtypeStruct(parts.shape[2:], jnp.bfloat16)
    whole = jax.ShapeDtypeStruct(attn.shape, jnp.bfloat16)
    return pl.pallas_call(
        keep_kernel,
        out_shape=[whole, whole, part, part],
        in_specs=[any_spec] * 3,
        out_specs=[any_spec] * 4,
        scratch_shapes=[pltpu.SemaphoreType.DMA((4, PIECES))],
        compiler_params=pltpu.CompilerParams(vmem_limit_bytes=1024 * 1024),
        name="keep",
    )(attn, query_grad, parts)


def body(head_dim, query_rows, key_rows, value_rows, grad_rows, doc_blocks, block_perm):
    attn, query_grad, parts = fused(
        head_dim, query_rows, grad_rows, key_rows, value_rows, doc_blocks, block_perm
    )
    if parts.shape[1] == 1:
        return keep(attn, query_grad, parts)
    parts = jnp.sum(parts.astype(jnp.float32), axis=1).astype(jnp.bfloat16)
    return attn, query_grad, parts[0], parts[1]


def solution(mesh):
    split = P(("ctx", "head"), None)
    out_spec = P("ctx", "head")
    return jax.shard_map(
        partial(body, mesh.shape["head"]),
        mesh=mesh,
        in_specs=(split, split, split, split, P(), P()),
        out_specs=(out_spec,) * 4,
        check_vma=False,
    )
```
